32 devices in a mesh: groups: 2 (over x), tile: 16 (over z, y, core).
Axes of the slice: x: 2, y: 2, z: 4, core: 2. Of those that a mesh axis runs over, the one named last changes fastest.
Arguments:
- grid_tokens: bfloat16 [16384, 512], P(('groups', 'tile')), parts along dimension 0, may hold values from -220 to 220
- obs_features: bfloat16 [65536, 128], P(('groups', 'tile')), parts along dimension 0, may hold values from -45 to 45
- w_obs: bfloat16 [128, 512], replicated, may hold values from -0.5 to 0.5
- b_obs: float32 [512], replicated, may hold values from -4 to 4
- w_query: bfloat16 [512, 512], replicated, may hold values from -0.25 to 0.25
- w_key: bfloat16 [512, 512], replicated, may hold values from -0.25 to 0.25
- w_value: bfloat16 [512, 512], replicated, may hold values from -0.25 to 0.25
- w_out: bfloat16 [512, 512], replicated, may hold values from -0.25 to 0.25
- block_lists: int32 [128, 32], P('groups'), parts along dimension 0, may hold values from 0 to 511, as said below
- block_counts: int32 [128], P('groups'), parts along dimension 0, may hold values from 24 to 32, as said below
- block_position: int32 [1024], P('groups'), parts along dimension 0, may hold values from 0 to 511, as said below
- proc_order: int32 [128], P('groups'), parts along dimension 0, may hold values from 0 to 63, each once
Outputs:
- arranged: bfloat16 [16384, 512], P(('groups', 'tile')), parts along dimension 0
The draws below stay inside these ranges and needn't reach their ends.
There are 2 independent parts, one for each index of `groups`. The reference program is written for one: setup_inputs(seed, part) draws one part's arguments, and reference() takes and returns one part's arrays. A program takes and returns all parts, laid end to end along the dimension named above; an argument that names none is the same for every part. Nothing has to cross between parts.
Inputs may be any that keep to these rules, and one draw needn't show every extreme that they name: `block_lists`: over the entries below block_counts of the 4 tiles t of one device (t // 4 equal), at most 16 name blocks whose storage position // 32 is any one device; in every draw some device has exactly 16 from some device. `block_counts`: some tile uses all 32 entries. `block_position`: A permutation of the storage positions.
All inputs are finite; a program needn't handle non-finite values.
Results may differ from the reference program's by a relative error of at most 0.012.
The reference program's roundings to bfloat16 on the way count: a program that leaves them out, or rounds other values in their place, can miss the bound.
Values may be sent and summed in bfloat16 or wider, within the bound.
A program may use at most 128 MiB of HBM per device.

```python
import math
import jax
import jax.numpy as jnp
from jax import lax

D = 512
FEAT = 128
HEADS = 8
BLOCK = 64
NSEL = 32
TILE_ROWS = 128
TILES_DEV = 4
OB_DEV = 32
TILES = 64
NBLK = 512
PIECE = 8
N_TILE = 16


def plan_blocks(key):
    position = jax.random.permutation(jax.random.fold_in(key, 101), NBLK).astype(jnp.int32)
    inverse = jnp.argsort(position).astype(jnp.int32)
    capacity = max(2, 2 * TILES_DEV * NSEL // N_TILE)
    entries = TILES_DEV * NSEL
    groups_needed = entries // capacity
    owner_keys = jax.random.split(jax.random.fold_in(key, 102), N_TILE)
    owner_perm = jax.vmap(lambda sub: jax.random.permutation(sub, N_TILE))(owner_keys)[:, :groups_needed]
    owner_dev = jnp.repeat(owner_perm.astype(jnp.int32), capacity, axis=1)
    local_blk = jax.random.randint(jax.random.fold_in(key, 103), (N_TILE, entries), 0, OB_DEV).astype(jnp.int32)
    blocks = jnp.take(inverse, owner_dev * OB_DEV + local_blk, axis=0).reshape(TILES, NSEL)
    shuffle_keys = jax.random.split(jax.random.fold_in(key, 104), TILES)
    shuffle = jax.vmap(lambda sub: jax.random.permutation(sub, NSEL))(shuffle_keys).astype(jnp.int32)
    lists = jnp.take_along_axis(blocks, shuffle, axis=1).astype(jnp.int32)
    counts = jax.random.randint(jax.random.fold_in(key, 105), (TILES,), 3 * NSEL // 4, NSEL + 1).astype(jnp.int32)
    full_tile = jax.random.randint(jax.random.fold_in(key, 106), (), 0, TILES)
    counts = jnp.where(jnp.arange(TILES) == full_tile, NSEL, counts).astype(jnp.int32)
    return (lists, counts, position)


def draw_block_lists(key, part):
    return plan_blocks(key)[0]


def draw_block_counts(key, part):
    return plan_blocks(key)[1]


def draw_block_position(key, part):
    return plan_blocks(key)[2]


def draw_grid_tokens(key, part):
    row_total = TILES * TILE_ROWS
    values = jnp.clip(jax.random.normal(jax.random.fold_in(key, 205), (row_total, D), jnp.float32), -6.0, 6.0)
    return values.astype(jnp.bfloat16)


def draw_obs_features(key, part):
    row_total = NBLK * BLOCK
    dev_rows = OB_DEV * BLOCK
    device_of_row = jnp.arange(row_total, dtype=jnp.int32) // dev_rows
    rise_pos = device_of_row.astype(jnp.float32)[:, None] / float(max(N_TILE - 1, 1))
    jitter = jnp.exp(jax.random.uniform(jax.random.fold_in(key, 306), (N_TILE, 1), jnp.float32, math.log(0.6), math.log(1.2)))
    dev_center = jax.random.uniform(jax.random.fold_in(key, 307), (N_TILE, FEAT), jnp.float32, -3.0, 3.0)
    blk_scale = jnp.exp(jax.random.uniform(jax.random.fold_in(key, 308), (NBLK, 1), jnp.float32, math.log(0.25), math.log(2.5)))
    spread = jnp.exp(jax.random.uniform(jax.random.fold_in(key, 301), (1, FEAT), jnp.float32, math.log(0.5), math.log(2.0)))
    row_jitter = jnp.repeat(jitter, dev_rows, axis=0)
    row_center = jnp.repeat(dev_center, dev_rows, axis=0)
    row_scale = jnp.repeat(blk_scale, BLOCK, axis=0)
    rise = 1.0 + 2.0 * rise_pos
    center = row_center
    noise = jnp.clip(jax.random.normal(jax.random.fold_in(key, 305), (row_total, FEAT), jnp.float32), -4.0, 4.0)
    values = rise * row_jitter * (center + row_scale * spread * noise)
    return jnp.clip(values, -45.0, 45.0).astype(jnp.bfloat16)


def gaussian(key, extent, scale, bound, kind=jnp.bfloat16):
    values = jax.random.normal(key, extent, jnp.float32) * scale
    return jnp.minimum(jnp.maximum(values, -bound), bound).astype(kind)


def setup_inputs(seed: int = 0, part: int = 0) -> dict:
    arg_keys = jax.random.split(jax.random.key(seed), 13)
    part_splits = jax.random.split(jax.random.fold_in(arg_keys[12], part), 13)
    return {
        "grid_tokens": draw_grid_tokens(jax.random.fold_in(jax.random.fold_in(arg_keys[12], part), 71), part),
        "obs_features": draw_obs_features(jax.random.fold_in(jax.random.fold_in(arg_keys[12], part), 71), part),
        "w_obs": gaussian(arg_keys[2], (FEAT, D), FEAT ** -0.5, 0.5),
        "b_obs": gaussian(arg_keys[3], (D,), 1.0, 4.0, jnp.float32),
        "w_query": gaussian(arg_keys[4], (D, D), D ** -0.5, 0.25),
        "w_key": gaussian(arg_keys[5], (D, D), D ** -0.5, 0.25),
        "w_value": gaussian(arg_keys[6], (D, D), D ** -0.5, 0.25),
        "w_out": gaussian(arg_keys[7], (D, D), D ** -0.5, 0.25),
        "block_lists": draw_block_lists(jax.random.fold_in(jax.random.fold_in(arg_keys[12], part), 71), part),
        "block_counts": draw_block_counts(jax.random.fold_in(jax.random.fold_in(arg_keys[12], part), 71), part),
        "block_position": draw_block_position(jax.random.fold_in(jax.random.fold_in(arg_keys[12], part), 71), part),
        "proc_order": jax.random.permutation(part_splits[11], TILES).astype(jnp.int32),
    }


def embed_rows(feats, feat_mean, feat_rstd, w_obs, b_obs):
    normed = ((feats.astype(jnp.float32) - feat_mean) * feat_rstd).astype(jnp.bfloat16)
    hidden = jnp.dot(normed, w_obs, preferred_element_type=jnp.float32) + b_obs
    return jax.nn.gelu(hidden, approximate=True).astype(jnp.bfloat16)

def reference(grid_tokens, obs_features, w_obs, b_obs, w_query, w_key, w_value, w_out, block_lists, block_counts, block_position, proc_order):
    obs_wide = obs_features.astype(jnp.float32)
    obs_total = obs_wide.shape[0]
    feat_mean = lax.optimization_barrier(jnp.sum(obs_wide, axis=0)) / obs_total
    second = lax.optimization_barrier(jnp.sum(obs_wide * obs_wide, axis=0)) / obs_total
    feat_rstd = lax.rsqrt(second - feat_mean * feat_mean + 1e-05)
    embedded = embed_rows(obs_features, feat_mean, feat_rstd, w_obs, b_obs)
    key_all = jnp.dot(embedded, w_key, preferred_element_type=jnp.float32).astype(jnp.bfloat16).reshape(NBLK, BLOCK, D)
    value_all = jnp.dot(embedded, w_value, preferred_element_type=jnp.float32).astype(jnp.bfloat16).reshape(NBLK, BLOCK, D)
    query_all = jnp.dot(grid_tokens, w_query, preferred_element_type=jnp.float32).astype(jnp.bfloat16).reshape(TILES, TILE_ROWS, D)
    head_dim = D // HEADS
    scale = 1.0 / head_dim ** 0.5

    def one_tile(items):
        query_tile, blocks, used = items
        spots = jnp.take(block_position, blocks, axis=0)
        key_tile = jnp.take(key_all, spots, axis=0).reshape(NSEL * BLOCK, HEADS, head_dim).astype(jnp.float32)
        value_tile = jnp.take(value_all, spots, axis=0).reshape(NSEL * BLOCK, HEADS, head_dim).astype(jnp.float32)
        query_wide = query_tile.reshape(TILE_ROWS, HEADS, head_dim).astype(jnp.float32)
        keymask = jnp.repeat(jnp.arange(NSEL, dtype=jnp.int32) < used, BLOCK)
        scores = jnp.einsum('qhd,khd->hqk', query_wide, key_tile) * scale
        scores = jnp.where(keymask[None, None, :], scores, jnp.float32(-1e+30))
        peak = lax.optimization_barrier(jnp.max(scores, axis=-1, keepdims=True))
        expo = jnp.exp(scores - peak)
        totals = lax.optimization_barrier(jnp.sum(expo, axis=-1))
        weights_bf = lax.optimization_barrier(expo.astype(jnp.bfloat16)).astype(jnp.float32)
        mixed = jnp.einsum('hqk,khd->qhd', weights_bf, value_tile)
        mixed = mixed / jnp.transpose(totals, (1, 0))[:, :, None]
        return mixed.reshape(TILE_ROWS, D).astype(jnp.bfloat16)
    attended = lax.map(one_tile, (query_all, block_lists, block_counts))
    encoded = jnp.dot(attended.reshape(TILES * TILE_ROWS, D), w_out, preferred_element_type=jnp.float32).astype(jnp.bfloat16)
    encoded = encoded.reshape(TILES, N_TILE, PIECE, D)
    placed = jnp.take(encoded, proc_order, axis=0)
    return jnp.transpose(placed, (1, 0, 2, 3)).reshape(TILES * TILE_ROWS, D)
```

```python
import functools

import jax
import jax.numpy as jnp
from jax import lax
from jax.experimental import pallas as pl
from jax.experimental.pallas import tpu as pltpu
from jax.sharding import PartitionSpec as P

HEADS = 8
BLOCK = 64
NSEL = 32
TILE_ROWS = 128
CHUNK = 512
NEG = -1e30


def attend_kernel(
    owned,
    list_ref,
    count_ref,
    position_ref,
    grid_ref,
    blocks_ref,
    mean_ref,
    rstd_ref,
    w_obs_ref,
    b_obs_ref,
    w_query_ref,
    w_key_ref,
    w_value_ref,
    w_out_ref,
    out_ref,
    raw,
    keys,
    values,
    copy_sem,
):
    tile = pl.program_id(0)
    tiles = pl.num_programs(0)
    key_span = NSEL * BLOCK
    width = grid_ref.shape[1]
    pair = 2 * (width // HEADS)
    base = lax.axis_index("tile") * tiles if owned else 0

    def fetch(which):
        slot = lax.rem(which, 2)

        def one(j, carry):
            spot = position_ref[list_ref[base + which, j]]
            pltpu.make_async_copy(
                blocks_ref.at[pl.ds(spot * BLOCK, BLOCK), :],
                raw.at[slot, pl.ds(j * BLOCK, BLOCK), :],
                copy_sem.at[slot],
            ).start()
            return carry

        lax.fori_loop(0, NSEL, one, 0)

    @pl.when(tile == 0)
    def _():
        fetch(tile)

    slot = lax.rem(tile, 2)
    pltpu.make_async_copy(
        blocks_ref.at[pl.ds(0, key_span), :], raw.at[slot], copy_sem.at[slot]
    ).wait()

    @pl.when(tile + 1 < tiles)
    def _():
        fetch(tile + 1)

    for start in range(0, key_span, CHUNK):
        rows = pl.ds(start, CHUNK)
        feats = raw[slot, rows, :].astype(jnp.float32)
        normed = ((feats - mean_ref[...]) * rstd_ref[...]).astype(jnp.bfloat16)
        hidden = jnp.dot(normed, w_obs_ref[...], preferred_element_type=jnp.float32)
        hidden = hidden + b_obs_ref[...]
        embedded = jax.nn.gelu(hidden, approximate=True).astype(jnp.bfloat16)
        keys[rows, :] = jnp.dot(
            embedded, w_key_ref[...], preferred_element_type=jnp.float32
        ).astype(jnp.bfloat16)
        values[rows, :] = jnp.dot(
            embedded, w_value_ref[...], preferred_element_type=jnp.float32
        ).astype(jnp.bfloat16)

    queries = jnp.dot(
        grid_ref[...], w_query_ref[...], preferred_element_type=jnp.float32
    ).astype(jnp.bfloat16)
    queries = queries * jnp.bfloat16(1.0 / (width // HEADS) ** 0.5)
    certain = 3 * key_span // 4
    used = count_ref[base + tile] * BLOCK
    key_index = certain + lax.broadcasted_iota(jnp.int32, (1, key_span - certain), 1)
    bias = jnp.where(key_index < used, 0.0, NEG).astype(jnp.float32)
    lane = lax.broadcasted_iota(jnp.int32, (TILE_ROWS, pair), 1)
    first = lane < pair // 2
    zero = jnp.zeros((), jnp.bfloat16)
    parts = []
    for p in range(HEADS // 2):
        columns = slice(p * pair, (p + 1) * pair)
        q = queries[:, columns]
        both = jnp.concatenate([jnp.where(first, q, zero), jnp.where(first, zero, q)], axis=0)
        scores = lax.dot_general(
            both,
            keys[:, columns],
            (((1,), (1,)), ((), ())),
            preferred_element_type=jnp.float32,
        )
        scores = jnp.concatenate([scores[:, :certain], scores[:, certain:] + bias], axis=1)
        peak = jnp.max(scores, axis=-1, keepdims=True)
        expo = jnp.exp(scores - peak)
        totals = jnp.sum(expo, axis=-1, keepdims=True)
        mixed = jnp.dot(
            expo.astype(jnp.bfloat16), values[:, columns], preferred_element_type=jnp.float32
        )
        mixed = mixed / totals
        parts.append(
            jnp.where(first, mixed[:TILE_ROWS], mixed[TILE_ROWS:]).astype(jnp.bfloat16)
        )
    attended = jnp.concatenate(parts, axis=1)
    encoded = jnp.dot(
        attended, w_out_ref[...], preferred_element_type=jnp.float32
    ).astype(jnp.bfloat16)
    out_ref[...] = encoded.reshape(out_ref.shape)


def attend(
    tile_count,
    owned,
    lists,
    counts,
    position,
    grid_tokens,
    blocks,
    mean,
    rstd,
    w_obs,
    b_obs,
    w_query,
    w_key,
    w_value,
    w_out,
):
    rows, width = grid_tokens.shape
    piece = TILE_ROWS // tile_count
    feat = blocks.shape[1]
    key_span = NSEL * BLOCK

    def whole(shape):
        return pl.BlockSpec(shape, lambda t, *_: (0, 0))

    square = whole((width, width))
    return pl.pallas_call(
        functools.partial(attend_kernel, owned),
        grid_spec=pltpu.PrefetchScalarGridSpec(
            num_scalar_prefetch=3,
            grid=(rows // TILE_ROWS,),
            in_specs=[
                pl.BlockSpec((TILE_ROWS, width), lambda t, *_: (t, 0)),
                pl.BlockSpec(memory_space=pl.ANY),
                whole((1, feat)),
                whole((1, feat)),
                whole((feat, width)),
                whole((1, width)),
                square,
                square,
                square,
                square,
            ],
            out_specs=pl.BlockSpec((tile_count, 1, piece, width), lambda t, *_: (0, t, 0, 0)),
            scratch_shapes=[
                pltpu.VMEM((2, key_span, feat), jnp.bfloat16),
                pltpu.VMEM((key_span, width), jnp.bfloat16),
                pltpu.VMEM((key_span, width), jnp.bfloat16),
                pltpu.SemaphoreType.DMA((2,)),
            ],
        ),
        out_shape=jax.ShapeDtypeStruct(
            (tile_count, rows // TILE_ROWS, piece, width), jnp.bfloat16
        ),
        compiler_params=pltpu.CompilerParams(dimension_semantics=("arbitrary",)),
        cost_estimate=pl.CostEstimate(
            flops=12_000_000_000, bytes_accessed=6_000_000, transcendentals=12_000_000
        ),
    )(
        lists,
        counts,
        position,
        grid_tokens,
        blocks,
        mean,
        rstd,
        w_obs,
        b_obs[None],
        w_query,
        w_key,
        w_value,
        w_out,
    )


MESH = pl.DeviceIdType.MESH


def greet_all(me, count):
    barrier = pltpu.get_barrier_semaphore()

    def one(k, carry):
        peer = lax.rem(me + k, count)
        pl.semaphore_signal(barrier, inc=1, device_id={"tile": peer}, device_id_type=MESH)
        return carry

    lax.fori_loop(1, count, one, 0)
    pl.semaphore_wait(barrier, count - 1)


LINES = 4
SIDES = LINES * 4
HALVES = 2
FIRST = 10
SECOND = 14
STEP = 8


def reorder(k, z):
    m = z // 2
    zz = z + m * (LINES - 1 - 2 * z)
    kk = k + zz * (1 - k // 2) * (1 - 2 * k)
    return kk + m * (LINES - 1 - 2 * kk)


def distance(zs, z):
    m = z // 2
    zz = z + m * (LINES - 1 - 2 * z)
    ss = zs + m * (LINES - 1 - 2 * zs)
    return ss + zz * (1 - ss // 2) * (1 - 2 * ss)


def plan_entries(me, lists_ref, count_ref, position_ref, plan, tiles, obs_blocks):
    entries = tiles * NSEL
    z, y, c = me // 4, lax.rem(me // 2, 2), lax.rem(me, 2)
    shift = obs_blocks.bit_length() - 1
    lane = lax.broadcasted_iota(jnp.int32, lists_ref.shape, 1)
    row = lax.broadcasted_iota(jnp.int32, (NSEL, 1), 0)
    ids, used = [], []
    for t in range(tiles):
        tile = me * tiles + t
        ids.append(jnp.sum(jnp.where(lane == tile, lists_ref[...], 0), axis=1, keepdims=True))
        used.append((row < count_ref[tile]).astype(jnp.int32))
    ids = jnp.concatenate(ids, axis=0)
    used = jnp.concatenate(used, axis=0)
    blocks = position_ref.shape[1]
    which = lax.broadcasted_iota(jnp.int32, (entries, blocks), 1)
    spot = jnp.sum(jnp.where(ids == which, position_ref[...], 0), axis=1, keepdims=True)
    owner = lax.shift_right_logical(spot, shift)
    inner = spot & (obs_blocks - 1)
    oz = lax.shift_right_logical(owner, 2)
    oy = lax.shift_right_logical(owner, 1) & 1
    near = jnp.zeros_like(oz)
    for zs in range(LINES):
        near = jnp.where(oz == zs, distance(zs, z), near)
    slot = near * 4 + (oy ^ y) * 2 + ((owner & 1) ^ c)
    slot = slot * used
    address = (slot * obs_blocks + inner) * used
    entry = lax.broadcasted_iota(jnp.int32, (entries, 1), 0)
    key = slot * entries + entry
    across = lax.broadcasted_iota(jnp.int32, (entries, entries), 1)
    down = lax.broadcasted_iota(jnp.int32, (entries, entries), 0)
    key_row = jnp.sum(jnp.where(across == down, key, 0), axis=0, keepdims=True)
    rank_row = jnp.sum((key < key_row).astype(jnp.int32), axis=0, keepdims=True)
    rank = jnp.sum((key_row < key).astype(jnp.int32), axis=1, keepdims=True)
    sorted_row = jnp.sum(jnp.where(rank == across, address, 0), axis=0, keepdims=True)
    plan[0:1, :] = rank_row
    plan[1:2, :] = sorted_row
    plan[2:3, :] = jnp.minimum(sorted_row, FIRST * obs_blocks - 1)
    behind = sorted_row - FIRST * obs_blocks
    plan[3:4, :] = jnp.minimum(jnp.maximum(behind, 0), (SECOND - FIRST) * obs_blocks - 1)


def fused_kernel(
    lists_ref,
    count_ref,
    position_ref,
    order_ref,
    grid_ref,
    obs_ref,
    w_obs_ref,
    b_obs_ref,
    w_query_ref,
    w_key_ref,
    w_value_ref,
    w_out_ref,
    out_ref,
    land,
    early,
    later,
    feed,
    keys,
    values,
    queries,
    encoded,
    arrived,
    plan,
    plan_s,
    part,
    parts,
    stats,
    sends,
    recvs,
    part_sends,
    part_recvs,
    out_sends,
    out_recvs,
    own_sems,
    stage_sems,
    plan_sem,
):
    count = SIDES
    me = lax.axis_index("tile")
    z, y, c = me // 4, lax.rem(me // 2, 2), lax.rem(me, 2)
    rows = obs_ref.shape[0]
    half = rows // HALVES
    tokens, width = grid_ref.shape
    tiles = tokens // TILE_ROWS
    obs_blocks = rows
    pair = 2 * (width // HEADS)
    order = [reorder(k, z) for k in range(LINES)]

    def index(zz, yy, cc):
        return (zz * 2 + yy) * 2 + cc

    def slot_of(zs, ys, cs, zt, yt, ct):
        dy = lax.rem(ys + yt, 2)
        dc = lax.rem(cs + ct, 2)
        return distance(zs, zt) * 4 + dy * 2 + dc

    def span(slot, h):
        return pl.ds(pl.multiple_of(slot * rows + h * half, half), half)

    def send(source, target, h, way, own=False):
        slot = slot_of(*source, *target)
        held = slot_of(*source, z, y, c)
        block = index(*source)
        return pltpu.make_async_remote_copy(
            src_ref=obs_ref.at[pl.ds(h * half, half)] if own else land.at[span(held, h)],
            dst_ref=land.at[span(slot, h)],
            send_sem=sends.at[way, HALVES * block + h],
            recv_sem=recvs.at[HALVES * block + h],
            device_id={"tile": index(*target)},
            device_id_type=MESH,
        )

    mine = (z, y, c)
    across = (z, 1 - y, c)
    beside = (z, y, 1 - c)
    started = []

    def launch(source, target, h, way, own=False, when=None):
        def issue(finish):
            def go():
                copy = send(source(), target(), h, way, own)
                copy.wait_send() if finish else copy.start()

            if when is None:
                go()
            else:
                pl.when(when())(go)

        started.append(issue)
        issue(False)

    def below_me():
        return z - 1, y, c

    def above_me():
        return z + 1, y, c

    def held_by_me():
        return mine

    def to_across():
        return across

    def to_beside():
        return beside

    def arrive(source, h):
        send(source, beside, h, 3).wait_recv()

    greet_all(me, count)
    for h in range(HALVES):
        launch(held_by_me, below_me, h, 0, True, lambda: z > 0)
        launch(held_by_me, above_me, h, 1, True, lambda: z < LINES - 1)
        launch(held_by_me, to_across, h, 2, True)
        launch(held_by_me, to_beside, h, 3, True)
    own_copies = [
        pltpu.make_async_copy(obs_ref, ref.at[pl.ds(0, rows)], own_sems.at[i])
        for i, ref in enumerate((land, early))
    ]
    for copy in own_copies:
        copy.start()

    feats = obs_ref[...].reshape(rows * BLOCK, obs_ref.shape[2]).astype(jnp.float32)
    part[...] = jnp.zeros_like(part)
    part[0:1, :] = jnp.sum(feats, axis=0, keepdims=True)
    part[1:2, :] = jnp.sum(feats * feats, axis=0, keepdims=True)
    parts[pl.ds(me, 1)] = part[...][None]

    def share_copy(k, source, peer):
        return pltpu.make_async_remote_copy(
            src_ref=part,
            dst_ref=parts.at[source],
            send_sem=part_sends.at[k],
            recv_sem=part_recvs.at[source],
            device_id={"tile": peer},
            device_id_type=MESH,
        )

    def share(k, carry):
        share_copy(k, me, lax.rem(me + k, count)).start()
        return carry

    lax.fori_loop(1, count, share, 0)

    plan_entries(me, lists_ref, count_ref, position_ref, plan, tiles, obs_blocks)
    plan_copy = pltpu.make_async_copy(plan, plan_s, plan_sem)
    plan_copy.start()
    queries[...] = jnp.dot(
        grid_ref[...], w_query_ref[...], preferred_element_type=jnp.float32
    ).astype(jnp.bfloat16) * jnp.bfloat16(1.0 / (width // HEADS) ** 0.5)
    plan_copy.wait()

    def column(k, h):
        def source():
            return order[k], y, c

        arrive(source(), h)
        launch(source, below_me, h, 0, False, lambda: (order[k] > z) & (z > 0))
        launch(source, above_me, h, 1, False, lambda: (order[k] < z) & (z < LINES - 1))
        if not (k == 1 and h == 1):
            launch(source, to_across, h, 2)
        launch(source, to_beside, h, 3)

    def opposite(k, h):
        def source():
            return order[k], 1 - y, c

        arrive(source(), h)
        if k == 0 and h == 1:
            launch(source, lambda: (order[1], y, c), h, 4)
        launch(source, to_beside, h, 3)

    def twin(k, dy, h):
        arrive((order[k], lax.rem(y + dy, 2), 1 - c), h)

    def stage(ref, sem, low, first, last):
        return pltpu.make_async_copy(
            land.at[pl.ds(first * rows, (last - first) * rows)],
            ref.at[pl.ds((first - low) * rows, (last - first) * rows)],
            stage_sems.at[sem],
        )

    for h in range(HALVES):
        column(1, h)
        opposite(0, h)
    for h in range(HALVES):
        twin(0, 0, h)
        twin(0, 1, h)
    stage(early, 0, 0, 1, 4).start()
    for h in range(HALVES):
        column(2, h)
        opposite(1, h)
    for h in range(HALVES):
        twin(1, 0, h)
    stage(early, 1, 0, 4, 6).start()
    for h in range(HALVES):
        twin(1, 1, h)
        twin(2, 0, h)
    stage(early, 2, 0, 6, FIRST).start()

    def gathered(k, carry):
        peer = lax.rem(me + k, count)
        share_copy(k, peer, peer).wait_send()
        share_copy(k, peer, peer).wait_recv()
        return carry

    lax.fori_loop(1, count, gathered, 0)
    sums = jnp.sum(parts[...], axis=0)
    total = rows * BLOCK * count
    mean = sums[0:1, :] / total
    stats[0:1, :] = mean
    stats[1:2, :] = lax.rsqrt(sums[1:2, :] / total - mean * mean + 1e-05)

    for copy in own_copies:
        copy.wait()
    stage(early, 0, 0, 1, 4).wait()
    stage(early, 1, 0, 4, 6).wait()
    stage(early, 2, 0, 6, FIRST).wait()

    chunk_rows = STEP * BLOCK
    chunks = tiles * NSEL // STEP
    share_of = chunks // 8

    def chunk(i, carry):
        @pl.when(i == share_of - 1)
        def _():
            column(3, 0)

        @pl.when(i == share_of)
        def _():
            opposite(2, 0)

        @pl.when(i == 2 * share_of - 1)
        def _():
            column(3, 1)

        @pl.when(i == 2 * share_of)
        def _():
            opposite(2, 1)
            for h in range(HALVES):
                twin(2, 1, h)
                twin(3, 0, h)
            stage(later, 3, FIRST, FIRST, SECOND).start()
            stage(later, 3, FIRST, FIRST, SECOND).wait()

        @pl.when(i == 4 * share_of)
        def _():
            opposite(3, 0)

        @pl.when(i == 5 * share_of)
        def _():
            opposite(3, 1)

        @pl.when(i == 6 * share_of)
        def _():
            for h in range(HALVES):
                twin(3, 1, h)

        @pl.when(i < 2 * share_of)
        def _():
            for u in range(STEP):
                feed[u] = early[plan_s[2, i * STEP + u]]

        @pl.when((i >= 2 * share_of) & (i < 6 * share_of))
        def _():
            for u in range(STEP):
                n = i * STEP + u
                spot = jnp.full(feed.shape[1:], plan_s[1, n], jnp.int32)
                feed[u] = jnp.where(
                    spot < FIRST * obs_blocks, early[plan_s[2, n]], later[plan_s[3, n]]
                )

        @pl.when(i >= 6 * share_of)
        def _():
            for u in range(STEP):
                feed[u] = land[plan_s[1, i * STEP + u]]

        feats = feed[...].reshape(chunk_rows, feed.shape[2]).astype(jnp.float32)
        normed = ((feats - stats[0:1, :]) * stats[1:2, :]).astype(jnp.bfloat16)
        hidden = jnp.dot(normed, w_obs_ref[...], preferred_element_type=jnp.float32)
        hidden = hidden + b_obs_ref[...]
        embedded = jax.nn.gelu(hidden, approximate=True).astype(jnp.bfloat16)
        place = pl.ds(i * STEP, STEP)
        key_rows = jnp.dot(embedded, w_key_ref[...], preferred_element_type=jnp.float32)
        keys[place] = key_rows.astype(jnp.bfloat16).reshape(STEP, BLOCK, width)
        value_rows = jnp.dot(embedded, w_value_ref[...], preferred_element_type=jnp.float32)
        values[place] = value_rows.astype(jnp.bfloat16).reshape(STEP, BLOCK, width)
        return carry

    lax.fori_loop(0, chunks, chunk, 0)

    key_span = NSEL * BLOCK
    certain = 3 * key_span // 4
    first = lax.broadcasted_iota(jnp.int32, (TILE_ROWS, pair), 1) < pair // 2
    zero = jnp.zeros((), jnp.bfloat16)
    piece = TILE_ROWS // count

    def out_copy(t, source, peer, k):
        return pltpu.make_async_remote_copy(
            src_ref=encoded.at[t, peer],
            dst_ref=arrived.at[source * tiles + t],
            send_sem=out_sends.at[t * count + k],
            recv_sem=out_recvs.at[source * tiles + t],
            device_id={"tile": peer},
            device_id_type=MESH,
        )

    def attend_tile(t, carry):
        used = count_ref[me * tiles + t] * BLOCK
        key_index = certain + lax.broadcasted_iota(jnp.int32, (1, key_span - certain), 1)
        bias = jnp.where(key_index < used, 0.0, NEG).astype(jnp.float32)
        places = [plan_s[0, t * NSEL + j] for j in range(NSEL)]
        outs = []
        for p in range(HEADS // 2):
            columns = slice(p * pair, (p + 1) * pair)
            q = queries[pl.ds(pl.multiple_of(t * TILE_ROWS, TILE_ROWS), TILE_ROWS), columns]
            both = jnp.concatenate([jnp.where(first, q, zero), jnp.where(first, zero, q)], axis=0)
            key_rows = jnp.concatenate([keys[place, :, columns] for place in places], axis=0)
            value_rows = jnp.concatenate([values[place, :, columns] for place in places], axis=0)
            scores = lax.dot_general(
                both, key_rows, (((1,), (1,)), ((), ())), preferred_element_type=jnp.float32
            )
            scores = jnp.concatenate([scores[:, :certain], scores[:, certain:] + bias], axis=1)
            peak = jnp.max(scores, axis=-1, keepdims=True)
            expo = jnp.exp(scores - peak)
            totals = jnp.sum(expo, axis=-1, keepdims=True)
            mixed = jnp.dot(
                expo.astype(jnp.bfloat16), value_rows, preferred_element_type=jnp.float32
            )
            mixed = mixed / totals
            outs.append(jnp.where(first, mixed[:TILE_ROWS], mixed[TILE_ROWS:]).astype(jnp.bfloat16))
        attended = jnp.concatenate(outs, axis=1)
        result = jnp.dot(attended, w_out_ref[...], preferred_element_type=jnp.float32)
        encoded[t] = result.astype(jnp.bfloat16).reshape(count, piece, width)

        def start(k, carry):
            out_copy(t, me, lax.rem(me + k, count), k).start()
            return carry

        lax.fori_loop(1, count, start, 0)
        arrived[pl.ds(me * tiles + t, 1)] = encoded[t, pl.ds(me, 1)]
        return carry

    lax.fori_loop(0, tiles, attend_tile, 0)

    for issue in started:
        issue(True)

    def finish(n, carry):
        t, k = n // (count - 1), 1 + lax.rem(n, count - 1)
        peer = lax.rem(me + k, count)
        out_copy(t, peer, peer, k).wait_send()
        out_copy(t, peer, peer, k).wait_recv()
        return carry

    lax.fori_loop(0, tiles * (count - 1), finish, 0)

    def arrange(j, carry):
        out_ref[pl.ds(j, 1)] = arrived[pl.ds(order_ref[j], 1)]
        return carry

    lax.fori_loop(0, count * tiles, arrange, 0, unroll=8)


def fused(lists, counts, position, proc_order, grid_tokens, obs_features, w_obs, b_obs, w_query, w_key, w_value, w_out):
    tokens, width = grid_tokens.shape
    rows, feat = obs_features.shape[0] // BLOCK, obs_features.shape[1]
    tiles = tokens // TILE_ROWS
    count = SIDES
    piece = TILE_ROWS // count
    entries = tiles * NSEL
    shape = (count * tiles, piece, width)
    vmem = pl.BlockSpec(memory_space=pltpu.VMEM)
    smem = pl.BlockSpec(memory_space=pltpu.SMEM)
    bf16 = jnp.bfloat16
    dma = pltpu.SemaphoreType.DMA
    return pl.pallas_call(
        fused_kernel,
        out_shape=jax.ShapeDtypeStruct(shape, bf16),
        in_specs=[vmem, smem, vmem, smem] + [vmem] * 8,
        out_specs=vmem,
        scratch_shapes=[
            pltpu.VMEM((SIDES * rows, BLOCK, feat), bf16),
            pltpu.VMEM((FIRST * rows, BLOCK, feat), bf16),
            pltpu.VMEM(((SECOND - FIRST) * rows, BLOCK, feat), bf16),
            pltpu.VMEM((STEP, BLOCK, feat), bf16),
            pltpu.VMEM((entries, BLOCK, width), bf16),
            pltpu.VMEM((entries, BLOCK, width), bf16),
            pltpu.VMEM((tokens, width), bf16),
            pltpu.VMEM((tiles, count, piece, width), bf16),
            pltpu.VMEM(shape, bf16),
            pltpu.VMEM((8, entries), jnp.int32),
            pltpu.SMEM((8, entries), jnp.int32),
            pltpu.VMEM((8, feat), jnp.float32),
            pltpu.VMEM((count, 8, feat), jnp.float32),
            pltpu.VMEM((8, feat), jnp.float32),
            dma((5, HALVES * count)),
            dma((HALVES * count,)),
            dma((count,)),
            dma((count,)),
            dma((tiles * count,)),
            dma((tiles * count,)),
            dma((2,)),
            dma((4,)),
            dma,
        ],
        compiler_params=pltpu.CompilerParams(
            collective_id=0, has_side_effects=True, vmem_limit_bytes=62 * 2**20
        ),
    )(
        lists.T,
        counts,
        position[None],
        proc_order,
        grid_tokens,
        obs_features.reshape(rows, BLOCK, feat),
        w_obs,
        b_obs[None],
        w_query,
        w_key,
        w_value,
        w_out,
    ).reshape(count * tiles * piece, width)


def exchange(obs_features, block_lists, block_counts, block_position, tile_count, own_index):
    obs_blocks = obs_features.shape[0] // BLOCK
    tile_local = block_lists.shape[0] // tile_count
    entry_count = tile_local * NSEL
    capacity = max(2, 2 * entry_count // tile_count)
    spots = jnp.take(block_position, block_lists, axis=0)
    is_valid = jnp.arange(NSEL, dtype=jnp.int32)[None, :] < block_counts[:, None]
    owner_dev = (spots // obs_blocks).reshape(tile_count, entry_count)
    local_blk = (spots % obs_blocks).reshape(tile_count, entry_count)
    valid_rows = is_valid.reshape(tile_count, entry_count)
    entry_order = jnp.arange(entry_count, dtype=jnp.int32)
    earlier = (
        (owner_dev[:, :, None] == owner_dev[:, None, :])
        & valid_rows[:, None, :]
        & (entry_order[None, :] < entry_order[:, None])[None, :, :]
    )
    slot_rank = jnp.sum(earlier.astype(jnp.int32), axis=2)
    mine = valid_rows & (owner_dev == own_index)
    slot_ids = jnp.arange(capacity, dtype=jnp.int32)
    hits = mine[:, None, :] & (slot_rank[:, None, :] == slot_ids[None, :, None])
    slot_block = jnp.sum(jnp.where(hits, local_blk[:, None, :], 0), axis=2)
    my_owner = lax.dynamic_index_in_dim(owner_dev, own_index, 0, keepdims=False)
    my_rank = lax.dynamic_index_in_dim(slot_rank, own_index, 0, keepdims=False)
    my_valid = lax.dynamic_index_in_dim(valid_rows, own_index, 0, keepdims=False)
    pick = jnp.where(my_valid, my_owner * capacity + my_rank, 0)
    raw_blocks = obs_features.reshape(obs_blocks, BLOCK, obs_features.shape[1])
    chosen = slot_block.reshape(-1, 1) == jnp.arange(obs_blocks, dtype=jnp.int32)[None, :]
    outgoing = jnp.einsum(
        "sb,brf->srf",
        chosen.astype(raw_blocks.dtype),
        raw_blocks,
        preferred_element_type=jnp.float32,
    ).astype(raw_blocks.dtype)
    incoming = lax.all_to_all(outgoing, "tile", split_axis=0, concat_axis=0, tiled=True)
    return incoming.reshape(tile_count * capacity * BLOCK, obs_features.shape[1]), pick


def local(
    grid_tokens,
    obs_features,
    w_obs,
    b_obs,
    w_query,
    w_key,
    w_value,
    w_out,
    block_lists,
    block_counts,
    block_position,
    proc_order,
):
    tile_count = lax.axis_size("tile")
    own_index = lax.axis_index("tile")
    tile_local = grid_tokens.shape[0] // TILE_ROWS
    width = grid_tokens.shape[1]
    if tile_count == SIDES:
        return fused(
            block_lists,
            block_counts,
            block_position,
            proc_order,
            grid_tokens,
            obs_features,
            w_obs,
            b_obs,
            w_query,
            w_key,
            w_value,
            w_out,
        )
    obs_wide = obs_features.astype(jnp.float32)
    first_sum, second_sum = lax.psum(
        (
            jnp.sum(obs_wide, axis=0, keepdims=True),
            jnp.sum(obs_wide * obs_wide, axis=0, keepdims=True),
        ),
        "tile",
    )
    obs_total = obs_features.shape[0] * tile_count
    feat_mean = first_sum / obs_total
    feat_rstd = lax.rsqrt(second_sum / obs_total - feat_mean * feat_mean + 1e-05)
    blocks, pick = exchange(
        obs_features, block_lists, block_counts, block_position, tile_count, own_index
    )
    encoded = attend(
        1,
        False,
        pick.reshape(tile_local, NSEL),
        lax.dynamic_slice_in_dim(block_counts, own_index * tile_local, tile_local),
        jnp.arange(blocks.shape[0] // BLOCK, dtype=jnp.int32),
        grid_tokens,
        blocks,
        feat_mean,
        feat_rstd,
        w_obs,
        b_obs,
        w_query,
        w_key,
        w_value,
        w_out,
    )
    outgoing = encoded.reshape(tile_local, tile_count, TILE_ROWS // tile_count, width)
    arrived = lax.all_to_all(outgoing, "tile", split_axis=1, concat_axis=0, tiled=True)
    arrived = arrived.reshape(tile_count * tile_local, TILE_ROWS // tile_count, width)
    return jnp.take(arrived, proc_order, axis=0).reshape(
        tile_count * tile_local * (TILE_ROWS // tile_count), width
    )


def solution(mesh):
    in_specs = (
        P(("groups", "tile"), None),
        P(("groups", "tile"), None),
        P(),
        P(),
        P(),
        P(),
        P(),
        P(),
        P("groups", None),
        P("groups"),
        P("groups"),
        P("groups"),
    )
    out_specs = P(("groups", "tile"), None)
    return jax.shard_map(local, mesh=mesh, in_specs=in_specs, out_specs=out_specs, check_vma=False)
```

```python
import functools

import jax
import jax.numpy as jnp
from jax import lax
from jax.experimental import pallas as pl
from jax.experimental.pallas import tpu as pltpu
from jax.sharding import PartitionSpec as P

HEADS = 8
BLOCK = 64
NSEL = 32
TILE_ROWS = 128
CHUNK = 512
NEG = -1e30


def attend_kernel(
    owned,
    list_ref,
    count_ref,
    position_ref,
    grid_ref,
    blocks_ref,
    mean_ref,
    rstd_ref,
    w_obs_ref,
    b_obs_ref,
    w_query_ref,
    w_key_ref,
    w_value_ref,
    w_out_ref,
    out_ref,
    raw,
    keys,
    values,
    copy_sem,
):
    tile = pl.program_id(0)
    tiles = pl.num_programs(0)
    key_span = NSEL * BLOCK
    width = grid_ref.shape[1]
    pair = 2 * (width // HEADS)
    base = lax.axis_index("tile") * tiles if owned else 0

    def fetch(which):
        slot = lax.rem(which, 2)

        def one(j, carry):
            spot = position_ref[list_ref[base + which, j]]
            pltpu.make_async_copy(
                blocks_ref.at[pl.ds(spot * BLOCK, BLOCK), :],
                raw.at[slot, pl.ds(j * BLOCK, BLOCK), :],
                copy_sem.at[slot],
            ).start()
            return carry

        lax.fori_loop(0, NSEL, one, 0)

    @pl.when(tile == 0)
    def _():
        fetch(tile)

    slot = lax.rem(tile, 2)
    pltpu.make_async_copy(
        blocks_ref.at[pl.ds(0, key_span), :], raw.at[slot], copy_sem.at[slot]
    ).wait()

    @pl.when(tile + 1 < tiles)
    def _():
        fetch(tile + 1)

    for start in range(0, key_span, CHUNK):
        rows = pl.ds(start, CHUNK)
        feats = raw[slot, rows, :].astype(jnp.float32)
        normed = ((feats - mean_ref[...]) * rstd_ref[...]).astype(jnp.bfloat16)
        hidden = jnp.dot(normed, w_obs_ref[...], preferred_element_type=jnp.float32)
        hidden = hidden + b_obs_ref[...]
        embedded = jax.nn.gelu(hidden, approximate=True).astype(jnp.bfloat16)
        keys[rows, :] = jnp.dot(
            embedded, w_key_ref[...], preferred_element_type=jnp.float32
        ).astype(jnp.bfloat16)
        values[rows, :] = jnp.dot(
            embedded, w_value_ref[...], preferred_element_type=jnp.float32
        ).astype(jnp.bfloat16)

    queries = jnp.dot(
        grid_ref[...], w_query_ref[...], preferred_element_type=jnp.float32
    ).astype(jnp.bfloat16)
    queries = queries * jnp.bfloat16(1.0 / (width // HEADS) ** 0.5)
    certain = 3 * key_span // 4
    used = count_ref[base + tile] * BLOCK
    key_index = certain + lax.broadcasted_iota(jnp.int32, (1, key_span - certain), 1)
    bias = jnp.where(key_index < used, 0.0, NEG).astype(jnp.float32)
    lane = lax.broadcasted_iota(jnp.int32, (TILE_ROWS, pair), 1)
    first = lane < pair // 2
    zero = jnp.zeros((), jnp.bfloat16)
    parts = []
    for p in range(HEADS // 2):
        columns = slice(p * pair, (p + 1) * pair)
        q = queries[:, columns]
        both = jnp.concatenate([jnp.where(first, q, zero), jnp.where(first, zero, q)], axis=0)
        scores = lax.dot_general(
            both,
            keys[:, columns],
            (((1,), (1,)), ((), ())),
            preferred_element_type=jnp.float32,
        )
        scores = jnp.concatenate([scores[:, :certain], scores[:, certain:] + bias], axis=1)
        peak = jnp.max(scores, axis=-1, keepdims=True)
        expo = jnp.exp(scores - peak)
        totals = jnp.sum(expo, axis=-1, keepdims=True)
        mixed = jnp.dot(
            expo.astype(jnp.bfloat16), values[:, columns], preferred_element_type=jnp.float32
        )
        mixed = mixed / totals
        parts.append(
            jnp.where(first, mixed[:TILE_ROWS], mixed[TILE_ROWS:]).astype(jnp.bfloat16)
        )
    attended = jnp.concatenate(parts, axis=1)
    encoded = jnp.dot(
        attended, w_out_ref[...], preferred_element_type=jnp.float32
    ).astype(jnp.bfloat16)
    out_ref[...] = encoded.reshape(out_ref.shape)


def attend(
    tile_count,
    owned,
    lists,
    counts,
    position,
    grid_tokens,
    blocks,
    mean,
    rstd,
    w_obs,
    b_obs,
    w_query,
    w_key,
    w_value,
    w_out,
):
    rows, width = grid_tokens.shape
    piece = TILE_ROWS // tile_count
    feat = blocks.shape[1]
    key_span = NSEL * BLOCK

    def whole(shape):
        return pl.BlockSpec(shape, lambda t, *_: (0, 0))

    square = whole((width, width))
    return pl.pallas_call(
        functools.partial(attend_kernel, owned),
        grid_spec=pltpu.PrefetchScalarGridSpec(
            num_scalar_prefetch=3,
            grid=(rows // TILE_ROWS,),
            in_specs=[
                pl.BlockSpec((TILE_ROWS, width), lambda t, *_: (t, 0)),
                pl.BlockSpec(memory_space=pl.ANY),
                whole((1, feat)),
                whole((1, feat)),
                whole((feat, width)),
                whole((1, width)),
                square,
                square,
                square,
                square,
            ],
            out_specs=pl.BlockSpec((tile_count, 1, piece, width), lambda t, *_: (0, t, 0, 0)),
            scratch_shapes=[
                pltpu.VMEM((2, key_span, feat), jnp.bfloat16),
                pltpu.VMEM((key_span, width), jnp.bfloat16),
                pltpu.VMEM((key_span, width), jnp.bfloat16),
                pltpu.SemaphoreType.DMA((2,)),
            ],
        ),
        out_shape=jax.ShapeDtypeStruct(
            (tile_count, rows // TILE_ROWS, piece, width), jnp.bfloat16
        ),
        compiler_params=pltpu.CompilerParams(dimension_semantics=("arbitrary",)),
        cost_estimate=pl.CostEstimate(
            flops=12_000_000_000, bytes_accessed=6_000_000, transcendentals=12_000_000
        ),
    )(
        lists,
        counts,
        position,
        grid_tokens,
        blocks,
        mean,
        rstd,
        w_obs,
        b_obs[None],
        w_query,
        w_key,
        w_value,
        w_out,
    )


MESH = pl.DeviceIdType.MESH


def greet_all(me, count):
    barrier = pltpu.get_barrier_semaphore()

    def one(k, carry):
        peer = lax.rem(me + k, count)
        pl.semaphore_signal(barrier, inc=1, device_id={"tile": peer}, device_id_type=MESH)
        return carry

    lax.fori_loop(1, count, one, 0)
    pl.semaphore_wait(barrier, count - 1)


LINES = 4
SIDES = LINES * 4
CORES = 2
PARTS = 1
STEP = 8


def reorder(k, z):
    m = z // 2
    zz = z + m * (LINES - 1 - 2 * z)
    kk = k + zz * (1 - k // 2) * (1 - 2 * k)
    return kk + m * (LINES - 1 - 2 * kk)


def distance(zs, z):
    m = z // 2
    zz = z + m * (LINES - 1 - 2 * z)
    ss = zs + m * (LINES - 1 - 2 * zs)
    return ss + zz * (1 - ss // 2) * (1 - 2 * ss)


def plan_entries(me, lists_ref, count_ref, position_ref, plan, tiles, obs_blocks):
    entries = tiles * NSEL
    z, y = me // 4, lax.rem(me // 2, 2)
    shift = obs_blocks.bit_length() - 1
    lane = lax.broadcasted_iota(jnp.int32, lists_ref.shape, 1)
    row = lax.broadcasted_iota(jnp.int32, (NSEL, 1), 0)
    ids, used = [], []
    for t in range(tiles):
        tile = me * tiles + t
        ids.append(jnp.sum(jnp.where(lane == tile, lists_ref[...], 0), axis=1, keepdims=True))
        used.append((row < count_ref[tile]).astype(jnp.int32))
    ids = jnp.concatenate(ids, axis=0)
    used = jnp.concatenate(used, axis=0)
    blocks = position_ref.shape[1]
    which = lax.broadcasted_iota(jnp.int32, (entries, blocks), 1)
    spot = jnp.sum(jnp.where(ids == which, position_ref[...], 0), axis=1, keepdims=True)
    owner = lax.shift_right_logical(spot, shift)
    inner = spot & (obs_blocks - 1)
    oz = lax.shift_right_logical(owner, 2)
    oy = lax.shift_right_logical(owner, 1) & 1
    near = jnp.zeros_like(oz)
    for zs in range(LINES):
        near = jnp.where(oz == zs, distance(zs, z), near)
    slot = near * 4 + (oy ^ y) * 2 + (owner & 1)
    address = (slot * obs_blocks + inner) * used
    turn = jnp.where(slot == 7, 14, jnp.where((slot > 7) & (slot < 15), slot - 1, slot)) * used
    entry = lax.broadcasted_iota(jnp.int32, (entries, 1), 0)
    key = turn * entries + entry
    across = lax.broadcasted_iota(jnp.int32, (entries, entries), 1)
    down = lax.broadcasted_iota(jnp.int32, (entries, entries), 0)
    key_row = jnp.sum(jnp.where(across == down, key, 0), axis=0, keepdims=True)
    rank_row = jnp.sum((key < key_row).astype(jnp.int32), axis=0, keepdims=True)
    rank = jnp.sum((key_row < key).astype(jnp.int32), axis=1, keepdims=True)
    sorted_row = jnp.sum(jnp.where(rank == across, address, 0), axis=0, keepdims=True)
    plan[0:1, :] = rank_row
    plan[1:2, :] = sorted_row


def fused_kernel(
    lists_ref,
    count_ref,
    position_ref,
    order_ref,
    b_obs_ref,
    obs_ref,
    grid_hbm,
    w_obs_hbm,
    w_query_hbm,
    w_key_hbm,
    w_value_hbm,
    w_out_hbm,
    out_ref,
    land,
    ready,
    feed,
    grid_ref,
    w_obs_ref,
    w_query_ref,
    w_key_ref,
    w_value_ref,
    w_out_ref,
    keys,
    values,
    queries,
    encoded,
    arrived,
    plan,
    plan_s,
    tally,
    tallies,
    stats,
    sends,
    recvs,
    part_sends,
    part_recvs,
    out_sends,
    out_recvs,
    own_sems,
    stage_sems,
    load_sems,
    plan_sem,
):
    count = SIDES
    me = lax.axis_index("tile")
    z, y, c = me // 4, lax.rem(me // 2, 2), lax.rem(me, 2)
    rows = obs_ref.shape[0]
    half = rows // CORES
    bit = half // PARTS
    tokens, width = grid_ref.shape
    tiles = tokens // TILE_ROWS
    obs_blocks = rows
    pair = 2 * (width // HEADS)
    order = [reorder(k, z) for k in range(LINES)]
    middle = (z > 0) & (z < LINES - 1)
    edge = jnp.logical_not(middle)

    loads = [
        pltpu.make_async_copy(source, target, load_sems.at[i])
        for i, (source, target) in enumerate(
            (
                (grid_hbm, grid_ref),
                (w_query_hbm, w_query_ref),
                (w_obs_hbm, w_obs_ref),
                (w_key_hbm, w_key_ref),
                (w_value_hbm, w_value_ref),
                (w_out_hbm, w_out_ref),
            )
        )
    ]
    own_place = pl.ds(pl.multiple_of(c * rows, rows), rows)
    own_copies = [
        pltpu.make_async_copy(obs_ref, ref.at[own_place], own_sems.at[i])
        for i, ref in enumerate((ready, land))
    ]

    def index(zz, yy, cc):
        return (zz * 2 + yy) * 2 + cc

    def slot_of(source, zt, yt):
        zs, ys, cs = source
        return distance(zs, zt) * 4 + lax.rem(ys + yt, 2) * 2 + cs

    def span(slot, side, part):
        return pl.ds(pl.multiple_of(slot * rows + side * half + part * bit, bit), bit)

    def send(source, target, side, part, way, own=False):
        block = index(*source)
        piece = (block * CORES + side) * PARTS + part
        return pltpu.make_async_remote_copy(
            src_ref=obs_ref.at[pl.ds(pl.multiple_of(side * half + part * bit, bit), bit)]
            if own
            else land.at[span(slot_of(source, z, y), side, part)],
            dst_ref=land.at[span(slot_of(source, target[0], target[1]), side, part)],
            send_sem=sends.at[way, piece],
            recv_sem=recvs.at[piece],
            device_id={"tile": index(*target)},
            device_id_type=MESH,
        )

    started = []

    def launch(source, target, side, part, way, own=False, when=None):
        def issue(finish):
            def go():
                copy = send(source(), target(), side(), part, way, own)
                copy.wait_send() if finish else copy.start()

            if when is None:
                go()
            else:
                pl.when(when())(go)

        started.append(issue)
        issue(False)

    def below_me():
        return z - 1, y, c

    def above_me():
        return z + 1, y, c

    def to_across():
        return z, 1 - y, c

    def to_beside():
        return z, y, 1 - c

    def my_side():
        return c

    def other_side():
        return 1 - c

    def arrive(source, side, part):
        send(source, to_beside(), side, part, 3).wait_recv()

    def spread(source, own, when):
        def both(cond):
            return cond if when is None else lambda: when() & cond()

        for part in range(PARTS):
            launch(source, below_me, my_side, part, 0, own, both(lambda: z > 0))
            launch(source, above_me, my_side, part, 1, own, both(lambda: z < LINES - 1))
            launch(source, to_across, my_side, part, 2, own, when)

    for copy in own_copies + loads:
        copy.start()
    greet_all(me, count)
    for part in range(PARTS):
        launch(lambda: (z, y, c), to_beside, other_side, part, 3, True)
    spread(lambda: (z, y, 0), True, lambda: c == 0)

    @pl.when(c == 1)
    def _():
        for part in range(PARTS):
            arrive((z, y, 0), c, part)

    spread(lambda: (z, y, 0), False, lambda: c == 1)

    @pl.when(c == 0)
    def _():
        for part in range(PARTS):
            arrive((z, y, 1), c, part)

    spread(lambda: (z, y, 1), False, lambda: c == 0)
    spread(lambda: (z, y, 1), True, lambda: c == 1)
    for part in range(PARTS):
        launch(lambda: (z, y, c), to_beside, my_side, part, 3, True)

    own_copies[0].wait()
    feats = ready[own_place].reshape(rows * BLOCK, obs_ref.shape[2]).astype(jnp.float32)
    tally[...] = jnp.zeros_like(tally)
    tally[0:1, :] = jnp.sum(feats, axis=0, keepdims=True)
    tally[1:2, :] = jnp.sum(feats * feats, axis=0, keepdims=True)
    tallies[pl.ds(me, 1)] = tally[...][None]

    def share_copy(k, source, peer):
        return pltpu.make_async_remote_copy(
            src_ref=tally,
            dst_ref=tallies.at[source],
            send_sem=part_sends.at[k],
            recv_sem=part_recvs.at[source],
            device_id={"tile": peer},
            device_id_type=MESH,
        )

    def share(k, carry):
        share_copy(k, me, lax.rem(me + k, count)).start()
        return carry

    lax.fori_loop(1, count, share, 0)

    plan_entries(me, lists_ref, count_ref, position_ref, plan, tiles, obs_blocks)
    plan_copy = pltpu.make_async_copy(plan, plan_s, plan_sem)
    plan_copy.start()
    loads[0].wait()
    loads[1].wait()
    queries[...] = jnp.dot(
        grid_ref[...], w_query_ref[...], preferred_element_type=jnp.float32
    ).astype(jnp.bfloat16) * jnp.bfloat16(1.0 / (width // HEADS) ** 0.5)
    plan_copy.wait()

    def column(k, cc):
        def source():
            return order[k], y, cc

        for part in range(PARTS):
            arrive(source(), c, part)
            launch(source, below_me, my_side, part, 0, False, lambda: (order[k] > z) & (z > 0))
            launch(source, above_me, my_side, part, 1, False, lambda: (order[k] < z) & (z < LINES - 1))
            if not (k == 1 and cc == 1):
                launch(source, to_across, my_side, part, 2)
            launch(source, to_beside, my_side, part, 3)

    def opposite(k, cc):
        def source():
            return order[k], 1 - y, cc

        for part in range(PARTS):
            arrive(source(), c, part)
            launch(source, to_beside, my_side, part, 3)

    def level():
        for part in range(PARTS):
            launch(lambda: (z, 1 - y, 1), lambda: (order[1], y, c), my_side, part, 4)

    def twin(k, dy, cc):
        for part in range(PARTS):
            arrive((order[k], lax.rem(y + dy, 2), cc), 1 - c, part)

    def kinds(inner, outer):
        kept = len(started)

        @pl.when(middle)
        def _():
            for event, args in inner:
                event(*args)

        del started[kept:]

        @pl.when(edge)
        def _():
            for event, args in outer:
                event(*args)

    def stage(sem, first, last):
        place = pl.ds(first * rows, (last - first) * rows)
        return pltpu.make_async_copy(land.at[place], ready.at[place], stage_sems.at[sem])

    for part in range(PARTS):
        arrive((z, y, 1 - c), 1 - c, part)
    beside_place = pl.ds(pl.multiple_of((1 - c) * rows, rows), rows)
    beside_copy = pltpu.make_async_copy(land.at[beside_place], ready.at[beside_place], stage_sems.at[0])
    beside_copy.start()
    columns = [(column, (1, 0)), (column, (1, 1)), (column, (2, 0)), (column, (2, 1))]
    columns += [(column, (3, 0)), (column, (3, 1))]
    across = [(opposite, (0, 0)), (opposite, (0, 1)), (opposite, (1, 0)), (opposite, (2, 0))]
    rebalance = (level, ())
    inner = [columns[0], columns[2], across[0], columns[1], columns[3], across[1]]
    inner += [columns[4], across[2], columns[5], rebalance, across[3]]
    outer = [columns[0], across[0], columns[1], across[1], rebalance]
    outer += [columns[2], across[2], columns[3], across[3]]
    kinds(inner, outer)
    for k, dy, cc in ((0, 1, 0), (0, 1, 1), (1, 0, 0), (1, 0, 1), (1, 1, 0)):
        twin(k, dy, cc)
    stage(1, 2, 7).start()
    for k, dy, cc in ((2, 0, 0), (2, 0, 1), (2, 1, 0)):
        twin(k, dy, cc)
    stage(2, 8, 11).start()

    def gathered(k, carry):
        peer = lax.rem(me + k, count)
        share_copy(k, peer, peer).wait_send()
        share_copy(k, peer, peer).wait_recv()
        return carry

    lax.fori_loop(1, count, gathered, 0)
    sums = jnp.sum(tallies[...], axis=0)
    total = rows * BLOCK * count
    mean = sums[0:1, :] / total
    stats[0:1, :] = mean
    stats[1:2, :] = lax.rsqrt(sums[1:2, :] / total - mean * mean + 1e-05)

    own_copies[1].wait()
    beside_copy.wait()
    stage(1, 2, 7).wait()
    stage(2, 8, 11).wait()
    for copy in loads[2:]:
        copy.wait()

    chunk_rows = STEP * BLOCK
    chunks = tiles * NSEL // STEP
    share_of = chunks // 4

    def advance(sem, first, last):
        copy = stage(sem, first, last)
        copy.start()
        copy.wait()

    def chunk(i, carry):
        @pl.when(i == share_of)
        def _():
            opposite(2, 1)
            kinds([], [columns[4]])
            twin(2, 1, 1)
            twin(3, 0, 0)
            advance(3, 11, 13)

        @pl.when(i == 2 * share_of)
        def _():
            kinds([], [columns[5]])
            opposite(3, 0)
            twin(3, 1, 0)
            twin(3, 0, 1)
            advance(4, 13, 15)

        @pl.when(i == 3 * share_of)
        def _():
            opposite(3, 1)
            opposite(1, 1)
            twin(3, 1, 1)
            twin(1, 1, 1)

        @pl.when(i < 3 * share_of)
        def _():
            for u in range(STEP):
                feed[u] = ready[plan_s[1, i * STEP + u]]

        @pl.when(i >= 3 * share_of)
        def _():
            for u in range(STEP):
                feed[u] = land[plan_s[1, i * STEP + u]]

        feats = feed[...].reshape(chunk_rows, feed.shape[2]).astype(jnp.float32)
        normed = ((feats - stats[0:1, :]) * stats[1:2, :]).astype(jnp.bfloat16)
        hidden = jnp.dot(normed, w_obs_ref[...], preferred_element_type=jnp.float32)
        hidden = hidden + b_obs_ref[...]
        embedded = jax.nn.gelu(hidden, approximate=True).astype(jnp.bfloat16)
        place = pl.ds(i * STEP, STEP)
        key_rows = jnp.dot(embedded, w_key_ref[...], preferred_element_type=jnp.float32)
        keys[place] = key_rows.astype(jnp.bfloat16).reshape(STEP, BLOCK, width)
        value_rows = jnp.dot(embedded, w_value_ref[...], preferred_element_type=jnp.float32)
        values[place] = value_rows.astype(jnp.bfloat16).reshape(STEP, BLOCK, width)
        return carry

    lax.fori_loop(0, chunks, chunk, 0)

    key_span = NSEL * BLOCK
    certain = 3 * key_span // 4
    first = lax.broadcasted_iota(jnp.int32, (TILE_ROWS, pair), 1) < pair // 2
    zero = jnp.zeros((), jnp.bfloat16)
    piece = TILE_ROWS // count

    def out_copy(t, source, peer, k):
        return pltpu.make_async_remote_copy(
            src_ref=encoded.at[t, peer],
            dst_ref=arrived.at[source * tiles + t],
            send_sem=out_sends.at[t * count + k],
            recv_sem=out_recvs.at[source * tiles + t],
            device_id={"tile": peer},
            device_id_type=MESH,
        )

    def attend_tile(t, carry):
        used = count_ref[me * tiles + t] * BLOCK
        key_index = certain + lax.broadcasted_iota(jnp.int32, (1, key_span - certain), 1)
        bias = jnp.where(key_index < used, 0.0, NEG).astype(jnp.float32)
        places = [plan_s[0, t * NSEL + j] for j in range(NSEL)]
        outs = []
        for p in range(HEADS // 2):
            columns = slice(p * pair, (p + 1) * pair)
            q = queries[pl.ds(pl.multiple_of(t * TILE_ROWS, TILE_ROWS), TILE_ROWS), columns]
            both = jnp.concatenate([jnp.where(first, q, zero), jnp.where(first, zero, q)], axis=0)
            key_rows = jnp.concatenate([keys[place, :, columns] for place in places], axis=0)
            value_rows = jnp.concatenate([values[place, :, columns] for place in places], axis=0)
            scores = lax.dot_general(
                both, key_rows, (((1,), (1,)), ((), ())), preferred_element_type=jnp.float32
            )
            scores = jnp.concatenate([scores[:, :certain], scores[:, certain:] + bias], axis=1)
            peak = jnp.max(scores, axis=-1, keepdims=True)
            expo = jnp.exp(scores - peak)
            totals = jnp.sum(expo, axis=-1, keepdims=True)
            mixed = jnp.dot(
                expo.astype(jnp.bfloat16), value_rows, preferred_element_type=jnp.float32
            )
            mixed = mixed / totals
            outs.append(jnp.where(first, mixed[:TILE_ROWS], mixed[TILE_ROWS:]).astype(jnp.bfloat16))
        attended = jnp.concatenate(outs, axis=1)
        result = jnp.dot(attended, w_out_ref[...], preferred_element_type=jnp.float32)
        encoded[t] = result.astype(jnp.bfloat16).reshape(count, piece, width)

        def start(k, carry):
            out_copy(t, me, lax.rem(me + k, count), k).start()
            return carry

        lax.fori_loop(1, count, start, 0)
        arrived[pl.ds(me * tiles + t, 1)] = encoded[t, pl.ds(me, 1)]
        return carry

    lax.fori_loop(0, tiles, attend_tile, 0)

    for issue in started:
        issue(True)

    def finish(n, carry):
        t, k = n // (count - 1), 1 + lax.rem(n, count - 1)
        peer = lax.rem(me + k, count)
        out_copy(t, peer, peer, k).wait_send()
        out_copy(t, peer, peer, k).wait_recv()
        return carry

    lax.fori_loop(0, tiles * (count - 1), finish, 0)

    def arrange(j, carry):
        out_ref[pl.ds(j, 1)] = arrived[pl.ds(order_ref[j], 1)]
        return carry

    lax.fori_loop(0, count * tiles, arrange, 0, unroll=8)


def fused(lists, counts, position, proc_order, grid_tokens, obs_features, w_obs, b_obs, w_query, w_key, w_value, w_out):
    tokens, width = grid_tokens.shape
    rows, feat = obs_features.shape[0] // BLOCK, obs_features.shape[1]
    tiles = tokens // TILE_ROWS
    count = SIDES
    piece = TILE_ROWS // count
    entries = tiles * NSEL
    shape = (count * tiles, piece, width)
    vmem = pl.BlockSpec(memory_space=pltpu.VMEM)
    smem = pl.BlockSpec(memory_space=pltpu.SMEM)
    bf16 = jnp.bfloat16
    dma = pltpu.SemaphoreType.DMA
    return pl.pallas_call(
        fused_kernel,
        out_shape=jax.ShapeDtypeStruct(shape, bf16),
        in_specs=[vmem, smem, vmem, smem, vmem] + [pl.BlockSpec(memory_space=pl.ANY)] * 7,
        out_specs=vmem,
        scratch_shapes=[
            pltpu.VMEM((SIDES * rows, BLOCK, feat), bf16),
            pltpu.VMEM(((SIDES - 1) * rows, BLOCK, feat), bf16),
            pltpu.VMEM((STEP, BLOCK, feat), bf16),
            pltpu.VMEM((tokens, width), bf16),
            pltpu.VMEM((feat, width), bf16),
            pltpu.VMEM((width, width), bf16),
            pltpu.VMEM((width, width), bf16),
            pltpu.VMEM((width, width), bf16),
            pltpu.VMEM((width, width), bf16),
            pltpu.VMEM((entries, BLOCK, width), bf16),
            pltpu.VMEM((entries, BLOCK, width), bf16),
            pltpu.VMEM((tokens, width), bf16),
            pltpu.VMEM((tiles, count, piece, width), bf16),
            pltpu.VMEM(shape, bf16),
            pltpu.VMEM((8, entries), jnp.int32),
            pltpu.SMEM((8, entries), jnp.int32),
            pltpu.VMEM((8, feat), jnp.float32),
            pltpu.VMEM((count, 8, feat), jnp.float32),
            pltpu.VMEM((8, feat), jnp.float32),
            dma((5, count * CORES * PARTS)),
            dma((count * CORES * PARTS,)),
            dma((count,)),
            dma((count,)),
            dma((tiles * count,)),
            dma((tiles * count,)),
            dma((2,)),
            dma((5,)),
            dma((6,)),
            dma,
        ],
        compiler_params=pltpu.CompilerParams(
            collective_id=0, has_side_effects=True, vmem_limit_bytes=62 * 2**20
        ),
    )(
        lists.T,
        counts,
        position[None],
        proc_order,
        b_obs[None],
        obs_features.reshape(rows, BLOCK, feat),
        grid_tokens,
        w_obs,
        w_query,
        w_key,
        w_value,
        w_out,
    ).reshape(count * tiles * piece, width)


def exchange(obs_features, block_lists, block_counts, block_position, tile_count, own_index):
    obs_blocks = obs_features.shape[0] // BLOCK
    tile_local = block_lists.shape[0] // tile_count
    entry_count = tile_local * NSEL
    capacity = max(2, 2 * entry_count // tile_count)
    spots = jnp.take(block_position, block_lists, axis=0)
    is_valid = jnp.arange(NSEL, dtype=jnp.int32)[None, :] < block_counts[:, None]
    owner_dev = (spots // obs_blocks).reshape(tile_count, entry_count)
    local_blk = (spots % obs_blocks).reshape(tile_count, entry_count)
    valid_rows = is_valid.reshape(tile_count, entry_count)
    entry_order = jnp.arange(entry_count, dtype=jnp.int32)
    earlier = (
        (owner_dev[:, :, None] == owner_dev[:, None, :])
        & valid_rows[:, None, :]
        & (entry_order[None, :] < entry_order[:, None])[None, :, :]
    )
    slot_rank = jnp.sum(earlier.astype(jnp.int32), axis=2)
    mine = valid_rows & (owner_dev == own_index)
    slot_ids = jnp.arange(capacity, dtype=jnp.int32)
    hits = mine[:, None, :] & (slot_rank[:, None, :] == slot_ids[None, :, None])
    slot_block = jnp.sum(jnp.where(hits, local_blk[:, None, :], 0), axis=2)
    my_owner = lax.dynamic_index_in_dim(owner_dev, own_index, 0, keepdims=False)
    my_rank = lax.dynamic_index_in_dim(slot_rank, own_index, 0, keepdims=False)
    my_valid = lax.dynamic_index_in_dim(valid_rows, own_index, 0, keepdims=False)
    pick = jnp.where(my_valid, my_owner * capacity + my_rank, 0)
    raw_blocks = obs_features.reshape(obs_blocks, BLOCK, obs_features.shape[1])
    chosen = slot_block.reshape(-1, 1) == jnp.arange(obs_blocks, dtype=jnp.int32)[None, :]
    outgoing = jnp.einsum(
        "sb,brf->srf",
        chosen.astype(raw_blocks.dtype),
        raw_blocks,
        preferred_element_type=jnp.float32,
    ).astype(raw_blocks.dtype)
    incoming = lax.all_to_all(outgoing, "tile", split_axis=0, concat_axis=0, tiled=True)
    return incoming.reshape(tile_count * capacity * BLOCK, obs_features.shape[1]), pick


def local(
    grid_tokens,
    obs_features,
    w_obs,
    b_obs,
    w_query,
    w_key,
    w_value,
    w_out,
    block_lists,
    block_counts,
    block_position,
    proc_order,
):
    tile_count = lax.axis_size("tile")
    own_index = lax.axis_index("tile")
    tile_local = grid_tokens.shape[0] // TILE_ROWS
    width = grid_tokens.shape[1]
    if tile_count == SIDES:
        return fused(
            block_lists,
            block_counts,
            block_position,
            proc_order,
            grid_tokens,
            obs_features,
            w_obs,
            b_obs,
            w_query,
            w_key,
            w_value,
            w_out,
        )
    obs_wide = obs_features.astype(jnp.float32)
    first_sum, second_sum = lax.psum(
        (
            jnp.sum(obs_wide, axis=0, keepdims=True),
            jnp.sum(obs_wide * obs_wide, axis=0, keepdims=True),
        ),
        "tile",
    )
    obs_total = obs_features.shape[0] * tile_count
    feat_mean = first_sum / obs_total
    feat_rstd = lax.rsqrt(second_sum / obs_total - feat_mean * feat_mean + 1e-05)
    blocks, pick = exchange(
        obs_features, block_lists, block_counts, block_position, tile_count, own_index
    )
    encoded = attend(
        1,
        False,
        pick.reshape(tile_local, NSEL),
        lax.dynamic_slice_in_dim(block_counts, own_index * tile_local, tile_local),
        jnp.arange(blocks.shape[0] // BLOCK, dtype=jnp.int32),
        grid_tokens,
        blocks,
        feat_mean,
        feat_rstd,
        w_obs,
        b_obs,
        w_query,
        w_key,
        w_value,
        w_out,
    )
    outgoing = encoded.reshape(tile_local, tile_count, TILE_ROWS // tile_count, width)
    arrived = lax.all_to_all(outgoing, "tile", split_axis=1, concat_axis=0, tiled=True)
    arrived = arrived.reshape(tile_count * tile_local, TILE_ROWS // tile_count, width)
    return jnp.take(arrived, proc_order, axis=0).reshape(
        tile_count * tile_local * (TILE_ROWS // tile_count), width
    )


def solution(mesh):
    in_specs = (
        P(("groups", "tile"), None),
        P(("groups", "tile"), None),
        P(),
        P(),
        P(),
        P(),
        P(),
        P(),
        P("groups", None),
        P("groups"),
        P("groups"),
        P("groups"),
    )
    out_specs = P(("groups", "tile"), None)
    return jax.shard_map(local, mesh=mesh, in_specs=in_specs, out_specs=out_specs, check_vma=False)
```

```python
import functools

import jax
import jax.numpy as jnp
from jax import lax
from jax.experimental import pallas as pl
from jax.experimental.pallas import tpu as pltpu
from jax.sharding import PartitionSpec as P

HEADS = 8
BLOCK = 64
NSEL = 32
TILE_ROWS = 128
CHUNK = 512
NEG = -1e30


def attend_kernel(
    owned,
    list_ref,
    count_ref,
    position_ref,
    grid_ref,
    blocks_ref,
    mean_ref,
    rstd_ref,
    w_obs_ref,
    b_obs_ref,
    w_query_ref,
    w_key_ref,
    w_value_ref,
    w_out_ref,
    out_ref,
    raw,
    keys,
    values,
    copy_sem,
):
    tile = pl.program_id(0)
    tiles = pl.num_programs(0)
    key_span = NSEL * BLOCK
    width = grid_ref.shape[1]
    pair = 2 * (width // HEADS)
    base = lax.axis_index("tile") * tiles if owned else 0

    def fetch(which):
        slot = lax.rem(which, 2)

        def one(j, carry):
            spot = position_ref[list_ref[base + which, j]]
            pltpu.make_async_copy(
                blocks_ref.at[pl.ds(spot * BLOCK, BLOCK), :],
                raw.at[slot, pl.ds(j * BLOCK, BLOCK), :],
                copy_sem.at[slot],
            ).start()
            return carry

        lax.fori_loop(0, NSEL, one, 0)

    @pl.when(tile == 0)
    def _():
        fetch(tile)

    slot = lax.rem(tile, 2)
    pltpu.make_async_copy(
        blocks_ref.at[pl.ds(0, key_span), :], raw.at[slot], copy_sem.at[slot]
    ).wait()

    @pl.when(tile + 1 < tiles)
    def _():
        fetch(tile + 1)

    for start in range(0, key_span, CHUNK):
        rows = pl.ds(start, CHUNK)
        feats = raw[slot, rows, :].astype(jnp.float32)
        normed = ((feats - mean_ref[...]) * rstd_ref[...]).astype(jnp.bfloat16)
        hidden = jnp.dot(normed, w_obs_ref[...], preferred_element_type=jnp.float32)
        hidden = hidden + b_obs_ref[...]
        embedded = jax.nn.gelu(hidden, approximate=True).astype(jnp.bfloat16)
        keys[rows, :] = jnp.dot(
            embedded, w_key_ref[...], preferred_element_type=jnp.float32
        ).astype(jnp.bfloat16)
        values[rows, :] = jnp.dot(
            embedded, w_value_ref[...], preferred_element_type=jnp.float32
        ).astype(jnp.bfloat16)

    queries = jnp.dot(
        grid_ref[...], w_query_ref[...], preferred_element_type=jnp.float32
    ).astype(jnp.bfloat16)
    queries = queries * jnp.bfloat16(1.0 / (width // HEADS) ** 0.5)
    certain = 3 * key_span // 4
    used = count_ref[base + tile] * BLOCK
    key_index = certain + lax.broadcasted_iota(jnp.int32, (1, key_span - certain), 1)
    bias = jnp.where(key_index < used, 0.0, NEG).astype(jnp.float32)
    lane = lax.broadcasted_iota(jnp.int32, (TILE_ROWS, pair), 1)
    first = lane < pair // 2
    zero = jnp.zeros((), jnp.bfloat16)
    parts = []
    for p in range(HEADS // 2):
        columns = slice(p * pair, (p + 1) * pair)
        q = queries[:, columns]
        both = jnp.concatenate([jnp.where(first, q, zero), jnp.where(first, zero, q)], axis=0)
        scores = lax.dot_general(
            both,
            keys[:, columns],
            (((1,), (1,)), ((), ())),
            preferred_element_type=jnp.float32,
        )
        scores = jnp.concatenate([scores[:, :certain], scores[:, certain:] + bias], axis=1)
        peak = jnp.max(scores, axis=-1, keepdims=True)
        expo = jnp.exp(scores - peak)
        totals = jnp.sum(expo, axis=-1, keepdims=True)
        mixed = jnp.dot(
            expo.astype(jnp.bfloat16), values[:, columns], preferred_element_type=jnp.float32
        )
        mixed = mixed / totals
        parts.append(
            jnp.where(first, mixed[:TILE_ROWS], mixed[TILE_ROWS:]).astype(jnp.bfloat16)
        )
    attended = jnp.concatenate(parts, axis=1)
    encoded = jnp.dot(
        attended, w_out_ref[...], preferred_element_type=jnp.float32
    ).astype(jnp.bfloat16)
    out_ref[...] = encoded.reshape(out_ref.shape)


def attend(
    tile_count,
    owned,
    lists,
    counts,
    position,
    grid_tokens,
    blocks,
    mean,
    rstd,
    w_obs,
    b_obs,
    w_query,
    w_key,
    w_value,
    w_out,
):
    rows, width = grid_tokens.shape
    piece = TILE_ROWS // tile_count
    feat = blocks.shape[1]
    key_span = NSEL * BLOCK

    def whole(shape):
        return pl.BlockSpec(shape, lambda t, *_: (0, 0))

    square = whole((width, width))
    return pl.pallas_call(
        functools.partial(attend_kernel, owned),
        grid_spec=pltpu.PrefetchScalarGridSpec(
            num_scalar_prefetch=3,
            grid=(rows // TILE_ROWS,),
            in_specs=[
                pl.BlockSpec((TILE_ROWS, width), lambda t, *_: (t, 0)),
                pl.BlockSpec(memory_space=pl.ANY),
                whole((1, feat)),
                whole((1, feat)),
                whole((feat, width)),
                whole((1, width)),
                square,
                square,
                square,
                square,
            ],
            out_specs=pl.BlockSpec((tile_count, 1, piece, width), lambda t, *_: (0, t, 0, 0)),
            scratch_shapes=[
                pltpu.VMEM((2, key_span, feat), jnp.bfloat16),
                pltpu.VMEM((key_span, width), jnp.bfloat16),
                pltpu.VMEM((key_span, width), jnp.bfloat16),
                pltpu.SemaphoreType.DMA((2,)),
            ],
        ),
        out_shape=jax.ShapeDtypeStruct(
            (tile_count, rows // TILE_ROWS, piece, width), jnp.bfloat16
        ),
        compiler_params=pltpu.CompilerParams(dimension_semantics=("arbitrary",)),
        cost_estimate=pl.CostEstimate(
            flops=12_000_000_000, bytes_accessed=6_000_000, transcendentals=12_000_000
        ),
    )(
        lists,
        counts,
        position,
        grid_tokens,
        blocks,
        mean,
        rstd,
        w_obs,
        b_obs[None],
        w_query,
        w_key,
        w_value,
        w_out,
    )


MESH = pl.DeviceIdType.MESH


def greet_all(me, count):
    barrier = pltpu.get_barrier_semaphore()

    def one(k, carry):
        peer = lax.rem(me + k, count)
        pl.semaphore_signal(barrier, inc=1, device_id={"tile": peer}, device_id_type=MESH)
        return carry

    lax.fori_loop(1, count, one, 0)
    pl.semaphore_wait(barrier, count - 1)


LINES = 4
SIDES = LINES * 4
CORES = 2
PARTS = 1
STEP = 32
SUB = 4


def reorder(k, z):
    m = z // 2
    zz = z + m * (LINES - 1 - 2 * z)
    kk = k + zz * (1 - k // 2) * (1 - 2 * k)
    return kk + m * (LINES - 1 - 2 * kk)


def distance(zs, z):
    m = z // 2
    zz = z + m * (LINES - 1 - 2 * z)
    ss = zs + m * (LINES - 1 - 2 * zs)
    return ss + zz * (1 - ss // 2) * (1 - 2 * ss)


def plan_entries(me, lists_ref, count_ref, position_ref, plan, tiles, obs_blocks):
    entries = tiles * NSEL
    z, y = me // 4, lax.rem(me // 2, 2)
    shift = obs_blocks.bit_length() - 1
    lane = lax.broadcasted_iota(jnp.int32, lists_ref.shape, 1)
    row = lax.broadcasted_iota(jnp.int32, (NSEL, 1), 0)
    ids, used = [], []
    for t in range(tiles):
        tile = me * tiles + t
        ids.append(jnp.sum(jnp.where(lane == tile, lists_ref[...], 0), axis=1, keepdims=True))
        used.append((row < count_ref[tile]).astype(jnp.int32))
    ids = jnp.concatenate(ids, axis=0)
    used = jnp.concatenate(used, axis=0)
    blocks = position_ref.shape[1]
    which = lax.broadcasted_iota(jnp.int32, (entries, blocks), 1)
    spot = jnp.sum(jnp.where(ids == which, position_ref[...], 0), axis=1, keepdims=True)
    owner = lax.shift_right_logical(spot, shift)
    inner = spot & (obs_blocks - 1)
    oz = lax.shift_right_logical(owner, 2)
    oy = lax.shift_right_logical(owner, 1) & 1
    near = jnp.zeros_like(oz)
    for zs in range(LINES):
        near = jnp.where(oz == zs, distance(zs, z), near)
    slot = near * 4 + (oy ^ y) * 2 + (owner & 1)
    address = (slot * obs_blocks + inner) * used
    turn = jnp.where(slot == 7, 14, jnp.where((slot > 7) & (slot < 15), slot - 1, slot)) * used
    entry = lax.broadcasted_iota(jnp.int32, (entries, 1), 0)
    key = turn * entries + entry
    across = lax.broadcasted_iota(jnp.int32, (entries, entries), 1)
    down = lax.broadcasted_iota(jnp.int32, (entries, entries), 0)
    key_row = jnp.sum(jnp.where(across == down, key, 0), axis=0, keepdims=True)
    rank_row = jnp.sum((key < key_row).astype(jnp.int32), axis=0, keepdims=True)
    rank = jnp.sum((key_row < key).astype(jnp.int32), axis=1, keepdims=True)
    sorted_row = jnp.sum(jnp.where(rank == across, address, 0), axis=0, keepdims=True)
    plan[0:1, :] = rank_row
    plan[1:2, :] = sorted_row


def fused_kernel(
    lists_ref,
    count_ref,
    position_ref,
    order_ref,
    b_obs_ref,
    obs_ref,
    grid_hbm,
    w_obs_hbm,
    w_query_hbm,
    w_key_hbm,
    w_value_hbm,
    w_out_hbm,
    out_ref,
    land,
    ready,
    feed,
    grid_ref,
    w_obs_ref,
    w_query_ref,
    w_key_ref,
    w_value_ref,
    w_out_ref,
    keys,
    values,
    queries,
    encoded,
    arrived,
    plan,
    plan_s,
    tally,
    tallies,
    stats,
    sends,
    recvs,
    part_sends,
    part_recvs,
    out_sends,
    out_recvs,
    own_sems,
    stage_sems,
    load_sems,
    plan_sem,
):
    count = SIDES
    me = lax.axis_index("tile")
    z, y, c = me // 4, lax.rem(me // 2, 2), lax.rem(me, 2)
    rows = obs_ref.shape[0]
    half = rows // CORES
    bit = half // PARTS
    tokens, width = grid_ref.shape
    tiles = tokens // TILE_ROWS
    obs_blocks = rows
    pair = 2 * (width // HEADS)
    order = [reorder(k, z) for k in range(LINES)]
    middle = (z > 0) & (z < LINES - 1)
    edge = jnp.logical_not(middle)

    loads = [
        pltpu.make_async_copy(source, target, load_sems.at[i])
        for i, (source, target) in enumerate(
            (
                (grid_hbm, grid_ref),
                (w_query_hbm, w_query_ref),
                (w_obs_hbm, w_obs_ref),
                (w_key_hbm, w_key_ref),
                (w_value_hbm, w_value_ref),
                (w_out_hbm, w_out_ref),
            )
        )
    ]
    own_place = pl.ds(pl.multiple_of(c * rows, rows), rows)
    own_copies = [
        pltpu.make_async_copy(obs_ref, ref.at[own_place], own_sems.at[i])
        for i, ref in enumerate((ready, land))
    ]

    def index(zz, yy, cc):
        return (zz * 2 + yy) * 2 + cc

    def slot_of(source, zt, yt):
        zs, ys, cs = source
        return distance(zs, zt) * 4 + lax.rem(ys + yt, 2) * 2 + cs

    def span(slot, side, part):
        return pl.ds(pl.multiple_of(slot * rows + side * half + part * bit, bit), bit)

    def send(source, target, side, part, way, own=False):
        block = index(*source)
        piece = (block * CORES + side) * PARTS + part
        return pltpu.make_async_remote_copy(
            src_ref=obs_ref.at[pl.ds(pl.multiple_of(side * half + part * bit, bit), bit)]
            if own
            else land.at[span(slot_of(source, z, y), side, part)],
            dst_ref=land.at[span(slot_of(source, target[0], target[1]), side, part)],
            send_sem=sends.at[way, piece],
            recv_sem=recvs.at[piece],
            device_id={"tile": index(*target)},
            device_id_type=MESH,
        )

    started = []

    def launch(source, target, side, part, way, own=False, when=None):
        def issue(finish):
            def go():
                copy = send(source(), target(), side(), part, way, own)
                copy.wait_send() if finish else copy.start()

            if when is None:
                go()
            else:
                pl.when(when())(go)

        started.append(issue)
        issue(False)

    def below_me():
        return z - 1, y, c

    def above_me():
        return z + 1, y, c

    def to_across():
        return z, 1 - y, c

    def to_beside():
        return z, y, 1 - c

    def my_side():
        return c

    def other_side():
        return 1 - c

    def arrive(source, side, part):
        send(source, to_beside(), side, part, 3).wait_recv()

    def spread(source, own, when):
        def both(cond):
            return cond if when is None else lambda: when() & cond()

        for part in range(PARTS):
            launch(source, below_me, my_side, part, 0, own, both(lambda: z > 0))
            launch(source, above_me, my_side, part, 1, own, both(lambda: z < LINES - 1))
            launch(source, to_across, my_side, part, 2, own, when)

    for copy in own_copies + loads:
        copy.start()
    greet_all(me, count)
    for part in range(PARTS):
        launch(lambda: (z, y, c), to_beside, other_side, part, 3, True)
    spread(lambda: (z, y, 0), True, lambda: c == 0)

    @pl.when(c == 1)
    def _():
        for part in range(PARTS):
            arrive((z, y, 0), c, part)

    spread(lambda: (z, y, 0), False, lambda: c == 1)

    @pl.when(c == 0)
    def _():
        for part in range(PARTS):
            arrive((z, y, 1), c, part)

    spread(lambda: (z, y, 1), False, lambda: c == 0)
    spread(lambda: (z, y, 1), True, lambda: c == 1)
    for part in range(PARTS):
        launch(lambda: (z, y, c), to_beside, my_side, part, 3, True)

    own_copies[0].wait()
    feats = ready[own_place].reshape(rows * BLOCK, obs_ref.shape[2]).astype(jnp.float32)
    tally[...] = jnp.zeros_like(tally)
    tally[0:1, :] = jnp.sum(feats, axis=0, keepdims=True)
    tally[1:2, :] = jnp.sum(feats * feats, axis=0, keepdims=True)
    tallies[pl.ds(me, 1)] = tally[...][None]

    def share_copy(k, source, peer):
        return pltpu.make_async_remote_copy(
            src_ref=tally,
            dst_ref=tallies.at[source],
            send_sem=part_sends.at[k],
            recv_sem=part_recvs.at[source],
            device_id={"tile": peer},
            device_id_type=MESH,
        )

    def share(k, carry):
        share_copy(k, me, lax.rem(me + k, count)).start()
        return carry

    lax.fori_loop(1, count, share, 0)

    plan_entries(me, lists_ref, count_ref, position_ref, plan, tiles, obs_blocks)
    plan_copy = pltpu.make_async_copy(plan, plan_s, plan_sem)
    plan_copy.start()
    loads[0].wait()
    loads[1].wait()
    queries[...] = jnp.dot(
        grid_ref[...], w_query_ref[...], preferred_element_type=jnp.float32
    ).astype(jnp.bfloat16) * jnp.bfloat16(1.0 / (width // HEADS) ** 0.5)
    plan_copy.wait()

    def column(k, cc):
        def source():
            return order[k], y, cc

        for part in range(PARTS):
            arrive(source(), c, part)
            launch(source, below_me, my_side, part, 0, False, lambda: (order[k] > z) & (z > 0))
            launch(source, above_me, my_side, part, 1, False, lambda: (order[k] < z) & (z < LINES - 1))
            if not (k == 1 and cc == 1):
                launch(source, to_across, my_side, part, 2)
            launch(source, to_beside, my_side, part, 3)

    def opposite(k, cc):
        def source():
            return order[k], 1 - y, cc

        for part in range(PARTS):
            arrive(source(), c, part)
            launch(source, to_beside, my_side, part, 3)

    def level():
        for part in range(PARTS):
            launch(lambda: (z, 1 - y, 1), lambda: (order[1], y, c), my_side, part, 4)

    def twin(k, dy, cc):
        for part in range(PARTS):
            arrive((order[k], lax.rem(y + dy, 2), cc), 1 - c, part)

    def kinds(inner, outer):
        kept = len(started)

        @pl.when(middle)
        def _():
            for event, args in inner:
                event(*args)

        del started[kept:]

        @pl.when(edge)
        def _():
            for event, args in outer:
                event(*args)

    def stage(sem, first, last):
        place = pl.ds(first * rows, (last - first) * rows)
        return pltpu.make_async_copy(land.at[place], ready.at[place], stage_sems.at[sem])

    for part in range(PARTS):
        arrive((z, y, 1 - c), 1 - c, part)
    beside_place = pl.ds(pl.multiple_of((1 - c) * rows, rows), rows)
    beside_copy = pltpu.make_async_copy(land.at[beside_place], ready.at[beside_place], stage_sems.at[0])
    beside_copy.start()
    columns = [(column, (1, 0)), (column, (1, 1)), (column, (2, 0)), (column, (2, 1))]
    columns += [(column, (3, 0)), (column, (3, 1))]
    across = [(opposite, (0, 0)), (opposite, (0, 1)), (opposite, (1, 0)), (opposite, (2, 0))]
    rebalance = (level, ())
    inner = [columns[0], columns[2], across[0], columns[1], columns[3], across[1]]
    inner += [columns[4], across[2], columns[5], rebalance, across[3]]
    outer = [columns[0], across[0], columns[1], across[1], rebalance]
    outer += [columns[2], across[2], columns[3], across[3]]
    kinds(inner, outer)
    for k, dy, cc in ((0, 1, 0), (0, 1, 1), (1, 0, 0), (1, 0, 1), (1, 1, 0)):
        twin(k, dy, cc)
    stage(1, 2, 7).start()
    for k, dy, cc in ((2, 0, 0), (2, 0, 1), (2, 1, 0)):
        twin(k, dy, cc)
    stage(2, 8, 11).start()

    def gathered(k, carry):
        peer = lax.rem(me + k, count)
        share_copy(k, peer, peer).wait_send()
        share_copy(k, peer, peer).wait_recv()
        return carry

    lax.fori_loop(1, count, gathered, 0)
    sums = jnp.sum(tallies[...], axis=0)
    total = rows * BLOCK * count
    mean = sums[0:1, :] / total
    stats[0:1, :] = mean
    stats[1:2, :] = lax.rsqrt(sums[1:2, :] / total - mean * mean + 1e-05)

    own_copies[1].wait()
    beside_copy.wait()
    stage(1, 2, 7).wait()
    stage(2, 8, 11).wait()
    for copy in loads[2:]:
        copy.wait()

    chunks = tiles * NSEL // STEP
    share_of = chunks // 4

    def advance(sem, first, last):
        copy = stage(sem, first, last)
        copy.start()
        copy.wait()

    def chunk(i, carry):
        @pl.when(i == share_of)
        def _():
            opposite(2, 1)
            kinds([], [columns[4]])
            twin(2, 1, 1)
            twin(3, 0, 0)
            advance(3, 11, 13)

        @pl.when(i == 2 * share_of)
        def _():
            kinds([], [columns[5]])
            opposite(3, 0)
            twin(3, 1, 0)
            twin(3, 0, 1)
            advance(4, 13, 15)

        @pl.when(i == 3 * share_of)
        def _():
            opposite(3, 1)
            opposite(1, 1)
            twin(3, 1, 1)
            twin(1, 1, 1)

        @pl.when(i < 3 * share_of)
        def _():
            for u in range(STEP):
                feed[u] = ready[plan_s[1, i * STEP + u]]

        @pl.when(i >= 3 * share_of)
        def _():
            for u in range(STEP):
                feed[u] = land[plan_s[1, i * STEP + u]]

        def embed(n):
            feats = feed[n * SUB : (n + 1) * SUB].reshape(SUB * BLOCK, feed.shape[2])
            normed = (feats.astype(jnp.float32) - stats[0:1, :]) * stats[1:2, :]
            hidden = jnp.dot(
                normed.astype(jnp.bfloat16), w_obs_ref[...], preferred_element_type=jnp.float32
            )
            hidden = hidden + b_obs_ref[...]
            return jax.nn.gelu(hidden, approximate=True).astype(jnp.bfloat16)

        ahead = embed(0)
        for n in range(STEP // SUB):
            embedded = ahead
            if n + 1 < STEP // SUB:
                ahead = embed(n + 1)
            place = pl.ds(i * STEP + n * SUB, SUB)
            key_rows = jnp.dot(embedded, w_key_ref[...], preferred_element_type=jnp.float32)
            keys[place] = key_rows.astype(jnp.bfloat16).reshape(SUB, BLOCK, width)
            value_rows = jnp.dot(embedded, w_value_ref[...], preferred_element_type=jnp.float32)
            values[place] = value_rows.astype(jnp.bfloat16).reshape(SUB, BLOCK, width)
        return carry

    lax.fori_loop(0, chunks, chunk, 0)

    key_span = NSEL * BLOCK
    certain = 3 * key_span // 4
    first = lax.broadcasted_iota(jnp.int32, (TILE_ROWS, pair), 1) < pair // 2
    zero = jnp.zeros((), jnp.bfloat16)
    piece = TILE_ROWS // count

    def out_copy(t, source, peer):
        return pltpu.make_async_remote_copy(
            src_ref=encoded.at[t, peer],
            dst_ref=arrived.at[source * tiles + t],
            send_sem=out_sends,
            recv_sem=out_recvs,
            device_id={"tile": peer},
            device_id_type=MESH,
        )

    def attend_tile(t, carry):
        used = count_ref[me * tiles + t] * BLOCK
        key_index = certain + lax.broadcasted_iota(jnp.int32, (1, key_span - certain), 1)
        bias = jnp.where(key_index < used, 0.0, NEG).astype(jnp.float32)
        places = [plan_s[0, t * NSEL + j] for j in range(NSEL)]
        outs = []

        def score(p):
            columns = slice(p * pair, (p + 1) * pair)
            q = queries[pl.ds(pl.multiple_of(t * TILE_ROWS, TILE_ROWS), TILE_ROWS), columns]
            both = jnp.concatenate([jnp.where(first, q, zero), jnp.where(first, zero, q)], axis=0)
            key_rows = jnp.concatenate([keys[place, :, columns] for place in places], axis=0)
            scores = lax.dot_general(
                both, key_rows, (((1,), (1,)), ((), ())), preferred_element_type=jnp.float32
            )
            return jnp.concatenate([scores[:, :certain], scores[:, certain:] + bias], axis=1)

        ahead = score(0)
        for p in range(HEADS // 2):
            scores = ahead
            if p + 1 < HEADS // 2:
                ahead = score(p + 1)
            columns = slice(p * pair, (p + 1) * pair)
            value_rows = jnp.concatenate([values[place, :, columns] for place in places], axis=0)
            value_rows = jnp.concatenate([value_rows, jnp.ones_like(value_rows)], axis=1)
            peak = jnp.max(scores, axis=-1, keepdims=True)
            expo = jnp.exp(scores - peak).astype(jnp.bfloat16)
            mixed = jnp.dot(expo, value_rows, preferred_element_type=jnp.float32)
            mixed = mixed[:, :pair] / mixed[:, pair:]
            outs.append(jnp.where(first, mixed[:TILE_ROWS], mixed[TILE_ROWS:]).astype(jnp.bfloat16))
        attended = jnp.concatenate(outs, axis=1)
        result = jnp.dot(attended, w_out_ref[...], preferred_element_type=jnp.float32)
        encoded[t] = result.astype(jnp.bfloat16).reshape(count, piece, width)

        def start(k, carry):
            out_copy(t, me, lax.rem(me + k, count)).start()
            return carry

        lax.fori_loop(1, count, start, 0)
        arrived[pl.ds(me * tiles + t, 1)] = encoded[t, pl.ds(me, 1)]
        return carry

    lax.fori_loop(0, tiles, attend_tile, 0)

    for issue in started:
        issue(True)

    for sem in (out_sends, out_recvs):
        moved = arrived.at[pl.ds(0, tiles * (count - 1))]
        pltpu.make_async_copy(moved, moved, sem).wait()

    def arrange(j, carry):
        out_ref[pl.ds(j, 1)] = arrived[pl.ds(order_ref[j], 1)]
        return carry

    lax.fori_loop(0, count * tiles, arrange, 0, unroll=8)


def fused(lists, counts, position, proc_order, grid_tokens, obs_features, w_obs, b_obs, w_query, w_key, w_value, w_out):
    tokens, width = grid_tokens.shape
    rows, feat = obs_features.shape[0] // BLOCK, obs_features.shape[1]
    tiles = tokens // TILE_ROWS
    count = SIDES
    piece = TILE_ROWS // count
    entries = tiles * NSEL
    shape = (count * tiles, piece, width)
    vmem = pl.BlockSpec(memory_space=pltpu.VMEM)
    smem = pl.BlockSpec(memory_space=pltpu.SMEM)
    bf16 = jnp.bfloat16
    dma = pltpu.SemaphoreType.DMA
    return pl.pallas_call(
        fused_kernel,
        out_shape=jax.ShapeDtypeStruct(shape, bf16),
        in_specs=[vmem, smem, vmem, smem, vmem] + [pl.BlockSpec(memory_space=pl.ANY)] * 7,
        out_specs=vmem,
        scratch_shapes=[
            pltpu.VMEM((SIDES * rows, BLOCK, feat), bf16),
            pltpu.VMEM(((SIDES - 1) * rows, BLOCK, feat), bf16),
            pltpu.VMEM((STEP, BLOCK, feat), bf16),
            pltpu.VMEM((tokens, width), bf16),
            pltpu.VMEM((feat, width), bf16),
            pltpu.VMEM((width, width), bf16),
            pltpu.VMEM((width, width), bf16),
            pltpu.VMEM((width, width), bf16),
            pltpu.VMEM((width, width), bf16),
            pltpu.VMEM((entries, BLOCK, width), bf16),
            pltpu.VMEM((entries, BLOCK, width), bf16),
            pltpu.VMEM((tokens, width), bf16),
            pltpu.VMEM((tiles, count, piece, width), bf16),
            pltpu.VMEM(shape, bf16),
            pltpu.VMEM((8, entries), jnp.int32),
            pltpu.SMEM((8, entries), jnp.int32),
            pltpu.VMEM((8, feat), jnp.float32),
            pltpu.VMEM((count, 8, feat), jnp.float32),
            pltpu.VMEM((8, feat), jnp.float32),
            dma((5, count * CORES * PARTS)),
            dma((count * CORES * PARTS,)),
            dma((count,)),
            dma((count,)),
            dma,
            dma,
            dma((2,)),
            dma((5,)),
            dma((6,)),
            dma,
        ],
        compiler_params=pltpu.CompilerParams(
            collective_id=0, has_side_effects=True, vmem_limit_bytes=62 * 2**20
        ),
    )(
        lists.T,
        counts,
        position[None],
        proc_order,
        b_obs[None],
        obs_features.reshape(rows, BLOCK, feat),
        grid_tokens,
        w_obs,
        w_query,
        w_key,
        w_value,
        w_out,
    ).reshape(count * tiles * piece, width)


def exchange(obs_features, block_lists, block_counts, block_position, tile_count, own_index):
    obs_blocks = obs_features.shape[0] // BLOCK
    tile_local = block_lists.shape[0] // tile_count
    entry_count = tile_local * NSEL
    capacity = max(2, 2 * entry_count // tile_count)
    spots = jnp.take(block_position, block_lists, axis=0)
    is_valid = jnp.arange(NSEL, dtype=jnp.int32)[None, :] < block_counts[:, None]
    owner_dev = (spots // obs_blocks).reshape(tile_count, entry_count)
    local_blk = (spots % obs_blocks).reshape(tile_count, entry_count)
    valid_rows = is_valid.reshape(tile_count, entry_count)
    entry_order = jnp.arange(entry_count, dtype=jnp.int32)
    earlier = (
        (owner_dev[:, :, None] == owner_dev[:, None, :])
        & valid_rows[:, None, :]
        & (entry_order[None, :] < entry_order[:, None])[None, :, :]
    )
    slot_rank = jnp.sum(earlier.astype(jnp.int32), axis=2)
    mine = valid_rows & (owner_dev == own_index)
    slot_ids = jnp.arange(capacity, dtype=jnp.int32)
    hits = mine[:, None, :] & (slot_rank[:, None, :] == slot_ids[None, :, None])
    slot_block = jnp.sum(jnp.where(hits, local_blk[:, None, :], 0), axis=2)
    my_owner = lax.dynamic_index_in_dim(owner_dev, own_index, 0, keepdims=False)
    my_rank = lax.dynamic_index_in_dim(slot_rank, own_index, 0, keepdims=False)
    my_valid = lax.dynamic_index_in_dim(valid_rows, own_index, 0, keepdims=False)
    pick = jnp.where(my_valid, my_owner * capacity + my_rank, 0)
    raw_blocks = obs_features.reshape(obs_blocks, BLOCK, obs_features.shape[1])
    chosen = slot_block.reshape(-1, 1) == jnp.arange(obs_blocks, dtype=jnp.int32)[None, :]
    outgoing = jnp.einsum(
        "sb,brf->srf",
        chosen.astype(raw_blocks.dtype),
        raw_blocks,
        preferred_element_type=jnp.float32,
    ).astype(raw_blocks.dtype)
    incoming = lax.all_to_all(outgoing, "tile", split_axis=0, concat_axis=0, tiled=True)
    return incoming.reshape(tile_count * capacity * BLOCK, obs_features.shape[1]), pick


def local(
    grid_tokens,
    obs_features,
    w_obs,
    b_obs,
    w_query,
    w_key,
    w_value,
    w_out,
    block_lists,
    block_counts,
    block_position,
    proc_order,
):
    tile_count = lax.axis_size("tile")
    own_index = lax.axis_index("tile")
    tile_local = grid_tokens.shape[0] // TILE_ROWS
    width = grid_tokens.shape[1]
    if tile_count == SIDES:
        return fused(
            block_lists,
            block_counts,
            block_position,
            proc_order,
            grid_tokens,
            obs_features,
            w_obs,
            b_obs,
            w_query,
            w_key,
            w_value,
            w_out,
        )
    obs_wide = obs_features.astype(jnp.float32)
    first_sum, second_sum = lax.psum(
        (
            jnp.sum(obs_wide, axis=0, keepdims=True),
            jnp.sum(obs_wide * obs_wide, axis=0, keepdims=True),
        ),
        "tile",
    )
    obs_total = obs_features.shape[0] * tile_count
    feat_mean = first_sum / obs_total
    feat_rstd = lax.rsqrt(second_sum / obs_total - feat_mean * feat_mean + 1e-05)
    blocks, pick = exchange(
        obs_features, block_lists, block_counts, block_position, tile_count, own_index
    )
    encoded = attend(
        1,
        False,
        pick.reshape(tile_local, NSEL),
        lax.dynamic_slice_in_dim(block_counts, own_index * tile_local, tile_local),
        jnp.arange(blocks.shape[0] // BLOCK, dtype=jnp.int32),
        grid_tokens,
        blocks,
        feat_mean,
        feat_rstd,
        w_obs,
        b_obs,
        w_query,
        w_key,
        w_value,
        w_out,
    )
    outgoing = encoded.reshape(tile_local, tile_count, TILE_ROWS // tile_count, width)
    arrived = lax.all_to_all(outgoing, "tile", split_axis=1, concat_axis=0, tiled=True)
    arrived = arrived.reshape(tile_count * tile_local, TILE_ROWS // tile_count, width)
    return jnp.take(arrived, proc_order, axis=0).reshape(
        tile_count * tile_local * (TILE_ROWS // tile_count), width
    )


def solution(mesh):
    in_specs = (
        P(("groups", "tile"), None),
        P(("groups", "tile"), None),
        P(),
        P(),
        P(),
        P(),
        P(),
        P(),
        P("groups", None),
        P("groups"),
        P("groups"),
        P("groups"),
    )
    out_specs = P(("groups", "tile"), None)
    return jax.shard_map(local, mesh=mesh, in_specs=in_specs, out_specs=out_specs, check_vma=False)
```

```python
import functools

import jax
import jax.numpy as jnp
from jax import lax
from jax.experimental import pallas as pl
from jax.experimental.pallas import tpu as pltpu
from jax.sharding import PartitionSpec as P

HEADS = 8
BLOCK = 64
NSEL = 32
TILE_ROWS = 128
CHUNK = 512
NEG = -1e30


def attend_kernel(
    owned,
    list_ref,
    count_ref,
    position_ref,
    grid_ref,
    blocks_ref,
    mean_ref,
    rstd_ref,
    w_obs_ref,
    b_obs_ref,
    w_query_ref,
    w_key_ref,
    w_value_ref,
    w_out_ref,
    out_ref,
    raw,
    keys,
    values,
    copy_sem,
):
    tile = pl.program_id(0)
    tiles = pl.num_programs(0)
    key_span = NSEL * BLOCK
    width = grid_ref.shape[1]
    pair = 2 * (width // HEADS)
    base = lax.axis_index("tile") * tiles if owned else 0

    def fetch(which):
        slot = lax.rem(which, 2)

        def one(j, carry):
            spot = position_ref[list_ref[base + which, j]]
            pltpu.make_async_copy(
                blocks_ref.at[pl.ds(spot * BLOCK, BLOCK), :],
                raw.at[slot, pl.ds(j * BLOCK, BLOCK), :],
                copy_sem.at[slot],
            ).start()
            return carry

        lax.fori_loop(0, NSEL, one, 0)

    @pl.when(tile == 0)
    def _():
        fetch(tile)

    slot = lax.rem(tile, 2)
    pltpu.make_async_copy(
        blocks_ref.at[pl.ds(0, key_span), :], raw.at[slot], copy_sem.at[slot]
    ).wait()

    @pl.when(tile + 1 < tiles)
    def _():
        fetch(tile + 1)

    for start in range(0, key_span, CHUNK):
        rows = pl.ds(start, CHUNK)
        feats = raw[slot, rows, :].astype(jnp.float32)
        normed = ((feats - mean_ref[...]) * rstd_ref[...]).astype(jnp.bfloat16)
        hidden = jnp.dot(normed, w_obs_ref[...], preferred_element_type=jnp.float32)
        hidden = hidden + b_obs_ref[...]
        embedded = jax.nn.gelu(hidden, approximate=True).astype(jnp.bfloat16)
        keys[rows, :] = jnp.dot(
            embedded, w_key_ref[...], preferred_element_type=jnp.float32
        ).astype(jnp.bfloat16)
        values[rows, :] = jnp.dot(
            embedded, w_value_ref[...], preferred_element_type=jnp.float32
        ).astype(jnp.bfloat16)

    queries = jnp.dot(
        grid_ref[...], w_query_ref[...], preferred_element_type=jnp.float32
    ).astype(jnp.bfloat16)
    queries = queries * jnp.bfloat16(1.0 / (width // HEADS) ** 0.5)
    certain = 3 * key_span // 4
    used = count_ref[base + tile] * BLOCK
    key_index = certain + lax.broadcasted_iota(jnp.int32, (1, key_span - certain), 1)
    bias = jnp.where(key_index < used, 0.0, NEG).astype(jnp.float32)
    lane = lax.broadcasted_iota(jnp.int32, (TILE_ROWS, pair), 1)
    first = lane < pair // 2
    zero = jnp.zeros((), jnp.bfloat16)
    parts = []
    for p in range(HEADS // 2):
        columns = slice(p * pair, (p + 1) * pair)
        q = queries[:, columns]
        both = jnp.concatenate([jnp.where(first, q, zero), jnp.where(first, zero, q)], axis=0)
        scores = lax.dot_general(
            both,
            keys[:, columns],
            (((1,), (1,)), ((), ())),
            preferred_element_type=jnp.float32,
        )
        scores = jnp.concatenate([scores[:, :certain], scores[:, certain:] + bias], axis=1)
        peak = jnp.max(scores, axis=-1, keepdims=True)
        expo = jnp.exp(scores - peak)
        totals = jnp.sum(expo, axis=-1, keepdims=True)
        mixed = jnp.dot(
            expo.astype(jnp.bfloat16), values[:, columns], preferred_element_type=jnp.float32
        )
        mixed = mixed / totals
        parts.append(
            jnp.where(first, mixed[:TILE_ROWS], mixed[TILE_ROWS:]).astype(jnp.bfloat16)
        )
    attended = jnp.concatenate(parts, axis=1)
    encoded = jnp.dot(
        attended, w_out_ref[...], preferred_element_type=jnp.float32
    ).astype(jnp.bfloat16)
    out_ref[...] = encoded.reshape(out_ref.shape)


def attend(
    tile_count,
    owned,
    lists,
    counts,
    position,
    grid_tokens,
    blocks,
    mean,
    rstd,
    w_obs,
    b_obs,
    w_query,
    w_key,
    w_value,
    w_out,
):
    rows, width = grid_tokens.shape
    piece = TILE_ROWS // tile_count
    feat = blocks.shape[1]
    key_span = NSEL * BLOCK

    def whole(shape):
        return pl.BlockSpec(shape, lambda t, *_: (0, 0))

    square = whole((width, width))
    return pl.pallas_call(
        functools.partial(attend_kernel, owned),
        grid_spec=pltpu.PrefetchScalarGridSpec(
            num_scalar_prefetch=3,
            grid=(rows // TILE_ROWS,),
            in_specs=[
                pl.BlockSpec((TILE_ROWS, width), lambda t, *_: (t, 0)),
                pl.BlockSpec(memory_space=pl.ANY),
                whole((1, feat)),
                whole((1, feat)),
                whole((feat, width)),
                whole((1, width)),
                square,
                square,
                square,
                square,
            ],
            out_specs=pl.BlockSpec((tile_count, 1, piece, width), lambda t, *_: (0, t, 0, 0)),
            scratch_shapes=[
                pltpu.VMEM((2, key_span, feat), jnp.bfloat16),
                pltpu.VMEM((key_span, width), jnp.bfloat16),
                pltpu.VMEM((key_span, width), jnp.bfloat16),
                pltpu.SemaphoreType.DMA((2,)),
            ],
        ),
        out_shape=jax.ShapeDtypeStruct(
            (tile_count, rows // TILE_ROWS, piece, width), jnp.bfloat16
        ),
        compiler_params=pltpu.CompilerParams(dimension_semantics=("arbitrary",)),
        cost_estimate=pl.CostEstimate(
            flops=12_000_000_000, bytes_accessed=6_000_000, transcendentals=12_000_000
        ),
    )(
        lists,
        counts,
        position,
        grid_tokens,
        blocks,
        mean,
        rstd,
        w_obs,
        b_obs[None],
        w_query,
        w_key,
        w_value,
        w_out,
    )


MESH = pl.DeviceIdType.MESH


def greet_all(me, count):
    barrier = pltpu.get_barrier_semaphore()

    def one(k, carry):
        peer = lax.rem(me + k, count)
        pl.semaphore_signal(barrier, inc=1, device_id={"tile": peer}, device_id_type=MESH)
        return carry

    lax.fori_loop(1, count, one, 0)
    pl.semaphore_wait(barrier, count - 1)


LINES = 4
SIDES = LINES * 4
CORES = 2
PARTS = 1
STEP = 32
SUB = 4


def reorder(k, z):
    m = z // 2
    zz = z + m * (LINES - 1 - 2 * z)
    kk = k + zz * (1 - k // 2) * (1 - 2 * k)
    return kk + m * (LINES - 1 - 2 * kk)


def distance(zs, z):
    m = z // 2
    zz = z + m * (LINES - 1 - 2 * z)
    ss = zs + m * (LINES - 1 - 2 * zs)
    return ss + zz * (1 - ss // 2) * (1 - 2 * ss)


def plan_entries(me, lists_ref, count_ref, position_ref, plan, tiles, obs_blocks):
    entries = tiles * NSEL
    z, y = me // 4, lax.rem(me // 2, 2)
    shift = obs_blocks.bit_length() - 1
    lane = lax.broadcasted_iota(jnp.int32, lists_ref.shape, 1)
    row = lax.broadcasted_iota(jnp.int32, (NSEL, 1), 0)
    ids, used = [], []
    for t in range(tiles):
        tile = me * tiles + t
        ids.append(jnp.sum(jnp.where(lane == tile, lists_ref[...], 0), axis=1, keepdims=True))
        used.append((row < count_ref[tile]).astype(jnp.int32))
    ids = jnp.concatenate(ids, axis=0)
    used = jnp.concatenate(used, axis=0)
    blocks = position_ref.shape[1]
    which = lax.broadcasted_iota(jnp.int32, (entries, blocks), 1)
    spot = jnp.sum(jnp.where(ids == which, position_ref[...], 0), axis=1, keepdims=True)
    owner = lax.shift_right_logical(spot, shift)
    inner = spot & (obs_blocks - 1)
    oz = lax.shift_right_logical(owner, 2)
    oy = lax.shift_right_logical(owner, 1) & 1
    near = jnp.zeros_like(oz)
    for zs in range(LINES):
        near = jnp.where(oz == zs, distance(zs, z), near)
    slot = near * 4 + (oy ^ y) * 2 + (owner & 1)
    address = (slot * obs_blocks + inner) * used
    turn = jnp.where(slot == 7, 14, jnp.where((slot > 7) & (slot < 15), slot - 1, slot)) * used
    entry = lax.broadcasted_iota(jnp.int32, (entries, 1), 0)
    key = turn * entries + entry
    across = lax.broadcasted_iota(jnp.int32, (entries, entries), 1)
    down = lax.broadcasted_iota(jnp.int32, (entries, entries), 0)
    key_row = jnp.sum(jnp.where(across == down, key, 0), axis=0, keepdims=True)
    rank_row = jnp.sum((key < key_row).astype(jnp.int32), axis=0, keepdims=True)
    rank = jnp.sum((key_row < key).astype(jnp.int32), axis=1, keepdims=True)
    sorted_row = jnp.sum(jnp.where(rank == across, address, 0), axis=0, keepdims=True)
    plan[0:1, :] = rank_row
    plan[1:2, :] = sorted_row


def fused_kernel(
    lists_hbm,
    count_hbm,
    position_hbm,
    b_obs_hbm,
    obs_ref,
    grid_hbm,
    w_obs_hbm,
    w_query_hbm,
    w_key_hbm,
    w_value_hbm,
    w_out_hbm,
    arrived,
    land,
    ready,
    feed,
    lists_ref,
    count_ref,
    position_ref,
    b_obs_ref,
    grid_ref,
    w_obs_ref,
    w_query_ref,
    w_key_ref,
    w_value_ref,
    w_out_ref,
    keys,
    values,
    queries,
    encoded,
    plan,
    plan_s,
    tally,
    tallies,
    stats,
    sends,
    recvs,
    part_sends,
    part_recvs,
    out_sends,
    out_recvs,
    own_sems,
    stage_sems,
    load_sems,
    plan_sem,
    kept_sems,
):
    count = SIDES
    me = lax.axis_index("tile")
    z, y, c = me // 4, lax.rem(me // 2, 2), lax.rem(me, 2)
    rows = obs_ref.shape[0]
    half = rows // CORES
    bit = half // PARTS
    tokens, width = grid_ref.shape
    tiles = tokens // TILE_ROWS
    obs_blocks = rows
    pair = 2 * (width // HEADS)
    order = [reorder(k, z) for k in range(LINES)]
    middle = (z > 0) & (z < LINES - 1)
    edge = jnp.logical_not(middle)

    loads = [
        pltpu.make_async_copy(source, target, load_sems.at[i])
        for i, (source, target) in enumerate(
            (
                (lists_hbm, lists_ref),
                (count_hbm, count_ref),
                (position_hbm, position_ref),
                (b_obs_hbm, b_obs_ref),
                (grid_hbm, grid_ref),
                (w_query_hbm, w_query_ref),
                (w_obs_hbm, w_obs_ref),
                (w_key_hbm, w_key_ref),
                (w_value_hbm, w_value_ref),
                (w_out_hbm, w_out_ref),
            )
        )
    ]
    own_place = pl.ds(pl.multiple_of(c * rows, rows), rows)
    own_copies = [
        pltpu.make_async_copy(obs_ref, ref.at[own_place], own_sems.at[i])
        for i, ref in enumerate((ready, land))
    ]

    def index(zz, yy, cc):
        return (zz * 2 + yy) * 2 + cc

    def slot_of(source, zt, yt):
        zs, ys, cs = source
        return distance(zs, zt) * 4 + lax.rem(ys + yt, 2) * 2 + cs

    def span(slot, side, part):
        return pl.ds(pl.multiple_of(slot * rows + side * half + part * bit, bit), bit)

    def send(source, target, side, part, way, own=False):
        block = index(*source)
        piece = (block * CORES + side) * PARTS + part
        return pltpu.make_async_remote_copy(
            src_ref=obs_ref.at[pl.ds(pl.multiple_of(side * half + part * bit, bit), bit)]
            if own
            else land.at[span(slot_of(source, z, y), side, part)],
            dst_ref=land.at[span(slot_of(source, target[0], target[1]), side, part)],
            send_sem=sends.at[way, piece],
            recv_sem=recvs.at[piece],
            device_id={"tile": index(*target)},
            device_id_type=MESH,
        )

    started = []

    def launch(source, target, side, part, way, own=False, when=None):
        def issue(finish):
            def go():
                copy = send(source(), target(), side(), part, way, own)
                copy.wait_send() if finish else copy.start()

            if when is None:
                go()
            else:
                pl.when(when())(go)

        started.append(issue)
        issue(False)

    def below_me():
        return z - 1, y, c

    def above_me():
        return z + 1, y, c

    def to_across():
        return z, 1 - y, c

    def to_beside():
        return z, y, 1 - c

    def my_side():
        return c

    def other_side():
        return 1 - c

    def arrive(source, side, part):
        send(source, to_beside(), side, part, 3).wait_recv()

    def spread(source, own, when):
        def both(cond):
            return cond if when is None else lambda: when() & cond()

        for part in range(PARTS):
            launch(source, below_me, my_side, part, 0, own, both(lambda: z > 0))
            launch(source, above_me, my_side, part, 1, own, both(lambda: z < LINES - 1))
            launch(source, to_across, my_side, part, 2, own, when)

    for copy in own_copies + loads:
        copy.start()
    greet_all(me, count)
    for part in range(PARTS):
        launch(lambda: (z, y, c), to_beside, other_side, part, 3, True)
    spread(lambda: (z, y, 0), True, lambda: c == 0)

    @pl.when(c == 1)
    def _():
        for part in range(PARTS):
            arrive((z, y, 0), c, part)

    spread(lambda: (z, y, 0), False, lambda: c == 1)

    @pl.when(c == 0)
    def _():
        for part in range(PARTS):
            arrive((z, y, 1), c, part)

    spread(lambda: (z, y, 1), False, lambda: c == 0)
    spread(lambda: (z, y, 1), True, lambda: c == 1)
    for part in range(PARTS):
        launch(lambda: (z, y, c), to_beside, my_side, part, 3, True)

    own_copies[0].wait()
    feats = ready[own_place].reshape(rows * BLOCK, obs_ref.shape[2]).astype(jnp.float32)
    tally[...] = jnp.zeros_like(tally)
    tally[0:1, :] = jnp.sum(feats, axis=0, keepdims=True)
    tally[1:2, :] = jnp.sum(feats * feats, axis=0, keepdims=True)
    tallies[pl.ds(me, 1)] = tally[...][None]

    def share_copy(k, source, peer):
        return pltpu.make_async_remote_copy(
            src_ref=tally,
            dst_ref=tallies.at[source],
            send_sem=part_sends.at[k],
            recv_sem=part_recvs.at[source],
            device_id={"tile": peer},
            device_id_type=MESH,
        )

    def share(k, carry):
        share_copy(k, me, lax.rem(me + k, count)).start()
        return carry

    lax.fori_loop(1, count, share, 0)

    for copy in loads[:6]:
        copy.wait()
    plan_entries(me, lists_ref, count_ref, position_ref, plan, tiles, obs_blocks)
    plan_copy = pltpu.make_async_copy(plan, plan_s, plan_sem)
    plan_copy.start()
    queries[...] = jnp.dot(
        grid_ref[...], w_query_ref[...], preferred_element_type=jnp.float32
    ).astype(jnp.bfloat16) * jnp.bfloat16(1.0 / (width // HEADS) ** 0.5)
    plan_copy.wait()

    def column(k, cc):
        def source():
            return order[k], y, cc

        for part in range(PARTS):
            arrive(source(), c, part)
            launch(source, below_me, my_side, part, 0, False, lambda: (order[k] > z) & (z > 0))
            launch(source, above_me, my_side, part, 1, False, lambda: (order[k] < z) & (z < LINES - 1))
            if not (k == 1 and cc == 1):
                launch(source, to_across, my_side, part, 2)
            launch(source, to_beside, my_side, part, 3)

    def opposite(k, cc):
        def source():
            return order[k], 1 - y, cc

        for part in range(PARTS):
            arrive(source(), c, part)
            launch(source, to_beside, my_side, part, 3)

    def level():
        for part in range(PARTS):
            launch(lambda: (z, 1 - y, 1), lambda: (order[1], y, c), my_side, part, 4)

    def twin(k, dy, cc):
        for part in range(PARTS):
            arrive((order[k], lax.rem(y + dy, 2), cc), 1 - c, part)

    def kinds(inner, outer):
        kept = len(started)

        @pl.when(middle)
        def _():
            for event, args in inner:
                event(*args)

        del started[kept:]

        @pl.when(edge)
        def _():
            for event, args in outer:
                event(*args)

    def stage(sem, first, last):
        place = pl.ds(first * rows, (last - first) * rows)
        return pltpu.make_async_copy(land.at[place], ready.at[place], stage_sems.at[sem])

    for part in range(PARTS):
        arrive((z, y, 1 - c), 1 - c, part)
    beside_place = pl.ds(pl.multiple_of((1 - c) * rows, rows), rows)
    beside_copy = pltpu.make_async_copy(land.at[beside_place], ready.at[beside_place], stage_sems.at[0])
    beside_copy.start()
    columns = [(column, (1, 0)), (column, (1, 1)), (column, (2, 0)), (column, (2, 1))]
    columns += [(column, (3, 0)), (column, (3, 1))]
    across = [(opposite, (0, 0)), (opposite, (0, 1)), (opposite, (1, 0)), (opposite, (2, 0))]
    rebalance = (level, ())
    inner = [columns[0], columns[2], across[0], columns[1], columns[3], across[1]]
    inner += [columns[4], across[2], columns[5], rebalance, across[3]]
    outer = [columns[0], across[0], columns[1], across[1], rebalance]
    outer += [columns[2], across[2], columns[3], across[3]]
    kinds(inner, outer)
    for k, dy, cc in ((0, 1, 0), (0, 1, 1), (1, 0, 0), (1, 0, 1), (1, 1, 0)):
        twin(k, dy, cc)
    stage(1, 2, 7).start()
    for k, dy, cc in ((2, 0, 0), (2, 0, 1), (2, 1, 0)):
        twin(k, dy, cc)
    stage(2, 8, 11).start()

    def gathered(k, carry):
        peer = lax.rem(me + k, count)
        share_copy(k, peer, peer).wait_send()
        share_copy(k, peer, peer).wait_recv()
        return carry

    lax.fori_loop(1, count, gathered, 0)
    sums = jnp.sum(tallies[...], axis=0)
    total = rows * BLOCK * count
    mean = sums[0:1, :] / total
    stats[0:1, :] = mean
    stats[1:2, :] = lax.rsqrt(sums[1:2, :] / total - mean * mean + 1e-05)

    own_copies[1].wait()
    beside_copy.wait()
    stage(1, 2, 7).wait()
    stage(2, 8, 11).wait()
    for copy in loads[6:]:
        copy.wait()

    chunks = tiles * NSEL // STEP
    share_of = chunks // 4

    def advance(sem, first, last):
        copy = stage(sem, first, last)
        copy.start()
        copy.wait()

    def chunk(i, carry):
        @pl.when(i == share_of)
        def _():
            opposite(2, 1)
            kinds([], [columns[4]])
            twin(2, 1, 1)
            twin(3, 0, 0)
            advance(3, 11, 13)

        @pl.when(i == 2 * share_of)
        def _():
            kinds([], [columns[5]])
            opposite(3, 0)
            twin(3, 1, 0)
            twin(3, 0, 1)
            advance(4, 13, 15)

        @pl.when(i == 3 * share_of)
        def _():
            opposite(3, 1)
            opposite(1, 1)
            twin(3, 1, 1)
            twin(1, 1, 1)

        @pl.when(i < 3 * share_of)
        def _():
            for u in range(STEP):
                feed[u] = ready[plan_s[1, i * STEP + u]]

        @pl.when(i >= 3 * share_of)
        def _():
            for u in range(STEP):
                feed[u] = land[plan_s[1, i * STEP + u]]

        def embed(n):
            feats = feed[n * SUB : (n + 1) * SUB].reshape(SUB * BLOCK, feed.shape[2])
            normed = (feats.astype(jnp.float32) - stats[0:1, :]) * stats[1:2, :]
            hidden = jnp.dot(
                normed.astype(jnp.bfloat16), w_obs_ref[...], preferred_element_type=jnp.float32
            )
            hidden = hidden + b_obs_ref[...]
            return jax.nn.gelu(hidden, approximate=True).astype(jnp.bfloat16)

        ahead = embed(0)
        for n in range(STEP // SUB):
            embedded = ahead
            if n + 1 < STEP // SUB:
                ahead = embed(n + 1)
            place = pl.ds(i * STEP + n * SUB, SUB)
            key_rows = jnp.dot(embedded, w_key_ref[...], preferred_element_type=jnp.float32)
            keys[place] = key_rows.astype(jnp.bfloat16).reshape(SUB, BLOCK, width)
            value_rows = jnp.dot(embedded, w_value_ref[...], preferred_element_type=jnp.float32)
            values[place] = value_rows.astype(jnp.bfloat16).reshape(SUB, BLOCK, width)
        return carry

    lax.fori_loop(0, chunks, chunk, 0)

    key_span = NSEL * BLOCK
    certain = 3 * key_span // 4
    first = lax.broadcasted_iota(jnp.int32, (TILE_ROWS, pair), 1) < pair // 2
    zero = jnp.zeros((), jnp.bfloat16)
    piece = TILE_ROWS // count

    def out_copy(t, source, peer):
        return pltpu.make_async_remote_copy(
            src_ref=encoded.at[t, peer],
            dst_ref=arrived.at[source * tiles + t],
            send_sem=out_sends,
            recv_sem=out_recvs,
            device_id={"tile": peer},
            device_id_type=MESH,
        )

    def kept_copy(t):
        return pltpu.make_async_copy(
            encoded.at[t, me], arrived.at[me * tiles + t], kept_sems.at[t]
        )

    def attend_tile(t, carry):
        used = count_ref[me * tiles + t] * BLOCK
        key_index = certain + lax.broadcasted_iota(jnp.int32, (1, key_span - certain), 1)
        bias = jnp.where(key_index < used, 0.0, NEG).astype(jnp.float32)
        places = [plan_s[0, t * NSEL + j] for j in range(NSEL)]
        outs = []

        def score(p):
            columns = slice(p * pair, (p + 1) * pair)
            q = queries[pl.ds(pl.multiple_of(t * TILE_ROWS, TILE_ROWS), TILE_ROWS), columns]
            both = jnp.concatenate([jnp.where(first, q, zero), jnp.where(first, zero, q)], axis=0)
            key_rows = jnp.concatenate([keys[place, :, columns] for place in places], axis=0)
            scores = lax.dot_general(
                both, key_rows, (((1,), (1,)), ((), ())), preferred_element_type=jnp.float32
            )
            return jnp.concatenate([scores[:, :certain], scores[:, certain:] + bias], axis=1)

        ahead = score(0)
        for p in range(HEADS // 2):
            scores = ahead
            if p + 1 < HEADS // 2:
                ahead = score(p + 1)
            columns = slice(p * pair, (p + 1) * pair)
            value_rows = jnp.concatenate([values[place, :, columns] for place in places], axis=0)
            value_rows = jnp.concatenate([value_rows, jnp.ones_like(value_rows)], axis=1)
            peak = jnp.max(scores, axis=-1, keepdims=True)
            expo = jnp.exp(scores - peak).astype(jnp.bfloat16)
            mixed = jnp.dot(expo, value_rows, preferred_element_type=jnp.float32)
            mixed = mixed[:, :pair] / mixed[:, pair:]
            outs.append(jnp.where(first, mixed[:TILE_ROWS], mixed[TILE_ROWS:]).astype(jnp.bfloat16))
        attended = jnp.concatenate(outs, axis=1)
        result = jnp.dot(attended, w_out_ref[...], preferred_element_type=jnp.float32)
        encoded[t] = result.astype(jnp.bfloat16).reshape(count, piece, width)

        def start(k, carry):
            out_copy(t, me, lax.rem(me + k, count)).start()
            return carry

        lax.fori_loop(1, count, start, 0)
        kept_copy(t).start()
        return carry

    lax.fori_loop(0, tiles, attend_tile, 0)

    for issue in started:
        issue(True)

    for sem in (out_sends, out_recvs):
        moved = arrived.at[pl.ds(0, tiles * (count - 1))]
        pltpu.make_async_copy(moved, moved, sem).wait()

    for t in range(tiles):
        kept_copy(t).wait()


def arrange_kernel(order_ref, arrived, out):
    for j in range(out.shape[0]):
        out[j] = arrived[order_ref[j]]


def arrange(arrived, proc_order):
    vmem = pl.BlockSpec(memory_space=pltpu.VMEM)
    return pl.pallas_call(
        arrange_kernel,
        out_shape=jax.ShapeDtypeStruct(arrived.shape, arrived.dtype),
        in_specs=[pl.BlockSpec(memory_space=pltpu.SMEM), vmem],
        out_specs=vmem,
    )(proc_order, arrived)


def fused(lists, counts, position, proc_order, grid_tokens, obs_features, w_obs, b_obs, w_query, w_key, w_value, w_out):
    tokens, width = grid_tokens.shape
    rows, feat = obs_features.shape[0] // BLOCK, obs_features.shape[1]
    tiles = tokens // TILE_ROWS
    count = SIDES
    piece = TILE_ROWS // count
    entries = tiles * NSEL
    shape = (count * tiles, piece, width)
    bf16 = jnp.bfloat16
    dma = pltpu.SemaphoreType.DMA
    arrived = pl.pallas_call(
        fused_kernel,
        out_shape=jax.ShapeDtypeStruct(shape, bf16),
        in_specs=[pl.BlockSpec(memory_space=pltpu.HBM)] * 11,
        out_specs=pl.BlockSpec(memory_space=pltpu.HBM),
        scratch_shapes=[
            pltpu.VMEM((SIDES * rows, BLOCK, feat), bf16),
            pltpu.VMEM(((SIDES - 1) * rows, BLOCK, feat), bf16),
            pltpu.VMEM((STEP, BLOCK, feat), bf16),
            pltpu.VMEM((NSEL, count * tiles), jnp.int32),
            pltpu.SMEM(counts.shape, jnp.int32),
            pltpu.VMEM((1, position.shape[0]), jnp.int32),
            pltpu.VMEM((1, width), jnp.float32),
            pltpu.VMEM((tokens, width), bf16),
            pltpu.VMEM((feat, width), bf16),
            pltpu.VMEM((width, width), bf16),
            pltpu.VMEM((width, width), bf16),
            pltpu.VMEM((width, width), bf16),
            pltpu.VMEM((width, width), bf16),
            pltpu.VMEM((entries, BLOCK, width), bf16),
            pltpu.VMEM((entries, BLOCK, width), bf16),
            pltpu.VMEM((tokens, width), bf16),
            pltpu.VMEM((tiles, count, piece, width), bf16),
            pltpu.VMEM((8, entries), jnp.int32),
            pltpu.SMEM((8, entries), jnp.int32),
            pltpu.VMEM((8, feat), jnp.float32),
            pltpu.VMEM((count, 8, feat), jnp.float32),
            pltpu.VMEM((8, feat), jnp.float32),
            dma((5, count * CORES * PARTS)),
            dma((count * CORES * PARTS,)),
            dma((count,)),
            dma((count,)),
            dma,
            dma,
            dma((2,)),
            dma((5,)),
            dma((10,)),
            dma,
            dma((tiles,)),
        ],
        compiler_params=pltpu.CompilerParams(
            collective_id=0, has_side_effects=True, vmem_limit_bytes=62 * 2**20
        ),
    )(
        lists.T,
        counts,
        position[None],
        b_obs[None],
        obs_features.reshape(rows, BLOCK, feat),
        grid_tokens,
        w_obs,
        w_query,
        w_key,
        w_value,
        w_out,
    )
    return arrange(arrived, proc_order).reshape(count * tiles * piece, width)


def exchange(obs_features, block_lists, block_counts, block_position, tile_count, own_index):
    obs_blocks = obs_features.shape[0] // BLOCK
    tile_local = block_lists.shape[0] // tile_count
    entry_count = tile_local * NSEL
    capacity = max(2, 2 * entry_count // tile_count)
    spots = jnp.take(block_position, block_lists, axis=0)
    is_valid = jnp.arange(NSEL, dtype=jnp.int32)[None, :] < block_counts[:, None]
    owner_dev = (spots // obs_blocks).reshape(tile_count, entry_count)
    local_blk = (spots % obs_blocks).reshape(tile_count, entry_count)
    valid_rows = is_valid.reshape(tile_count, entry_count)
    entry_order = jnp.arange(entry_count, dtype=jnp.int32)
    earlier = (
        (owner_dev[:, :, None] == owner_dev[:, None, :])
        & valid_rows[:, None, :]
        & (entry_order[None, :] < entry_order[:, None])[None, :, :]
    )
    slot_rank = jnp.sum(earlier.astype(jnp.int32), axis=2)
    mine = valid_rows & (owner_dev == own_index)
    slot_ids = jnp.arange(capacity, dtype=jnp.int32)
    hits = mine[:, None, :] & (slot_rank[:, None, :] == slot_ids[None, :, None])
    slot_block = jnp.sum(jnp.where(hits, local_blk[:, None, :], 0), axis=2)
    my_owner = lax.dynamic_index_in_dim(owner_dev, own_index, 0, keepdims=False)
    my_rank = lax.dynamic_index_in_dim(slot_rank, own_index, 0, keepdims=False)
    my_valid = lax.dynamic_index_in_dim(valid_rows, own_index, 0, keepdims=False)
    pick = jnp.where(my_valid, my_owner * capacity + my_rank, 0)
    raw_blocks = obs_features.reshape(obs_blocks, BLOCK, obs_features.shape[1])
    chosen = slot_block.reshape(-1, 1) == jnp.arange(obs_blocks, dtype=jnp.int32)[None, :]
    outgoing = jnp.einsum(
        "sb,brf->srf",
        chosen.astype(raw_blocks.dtype),
        raw_blocks,
        preferred_element_type=jnp.float32,
    ).astype(raw_blocks.dtype)
    incoming = lax.all_to_all(outgoing, "tile", split_axis=0, concat_axis=0, tiled=True)
    return incoming.reshape(tile_count * capacity * BLOCK, obs_features.shape[1]), pick


def local(
    grid_tokens,
    obs_features,
    w_obs,
    b_obs,
    w_query,
    w_key,
    w_value,
    w_out,
    block_lists,
    block_counts,
    block_position,
    proc_order,
):
    tile_count = lax.axis_size("tile")
    own_index = lax.axis_index("tile")
    tile_local = grid_tokens.shape[0] // TILE_ROWS
    width = grid_tokens.shape[1]
    if tile_count == SIDES:
        return fused(
            block_lists,
            block_counts,
            block_position,
            proc_order,
            grid_tokens,
            obs_features,
            w_obs,
            b_obs,
            w_query,
            w_key,
            w_value,
            w_out,
        )
    obs_wide = obs_features.astype(jnp.float32)
    first_sum, second_sum = lax.psum(
        (
            jnp.sum(obs_wide, axis=0, keepdims=True),
            jnp.sum(obs_wide * obs_wide, axis=0, keepdims=True),
        ),
        "tile",
    )
    obs_total = obs_features.shape[0] * tile_count
    feat_mean = first_sum / obs_total
    feat_rstd = lax.rsqrt(second_sum / obs_total - feat_mean * feat_mean + 1e-05)
    blocks, pick = exchange(
        obs_features, block_lists, block_counts, block_position, tile_count, own_index
    )
    encoded = attend(
        1,
        False,
        pick.reshape(tile_local, NSEL),
        lax.dynamic_slice_in_dim(block_counts, own_index * tile_local, tile_local),
        jnp.arange(blocks.shape[0] // BLOCK, dtype=jnp.int32),
        grid_tokens,
        blocks,
        feat_mean,
        feat_rstd,
        w_obs,
        b_obs,
        w_query,
        w_key,
        w_value,
        w_out,
    )
    outgoing = encoded.reshape(tile_local, tile_count, TILE_ROWS // tile_count, width)
    arrived = lax.all_to_all(outgoing, "tile", split_axis=1, concat_axis=0, tiled=True)
    arrived = arrived.reshape(tile_count * tile_local, TILE_ROWS // tile_count, width)
    return jnp.take(arrived, proc_order, axis=0).reshape(
        tile_count * tile_local * (TILE_ROWS // tile_count), width
    )


def solution(mesh):
    in_specs = (
        P(("groups", "tile"), None),
        P(("groups", "tile"), None),
        P(),
        P(),
        P(),
        P(),
        P(),
        P(),
        P("groups", None),
        P("groups"),
        P("groups"),
        P("groups"),
    )
    out_specs = P(("groups", "tile"), None)
    return jax.shard_map(local, mesh=mesh, in_specs=in_specs, out_specs=out_specs, check_vma=False)
```

```python
import functools

import jax
import jax.numpy as jnp
from jax import lax
from jax.experimental import pallas as pl
from jax.experimental.pallas import tpu as pltpu
from jax.sharding import PartitionSpec as P

HEADS = 8
BLOCK = 64
NSEL = 32
TILE_ROWS = 128
CHUNK = 512
NEG = -1e30


def attend_kernel(
    owned,
    list_ref,
    count_ref,
    position_ref,
    grid_ref,
    blocks_ref,
    mean_ref,
    rstd_ref,
    w_obs_ref,
    b_obs_ref,
    w_query_ref,
    w_key_ref,
    w_value_ref,
    w_out_ref,
    out_ref,
    raw,
    keys,
    values,
    copy_sem,
):
    tile = pl.program_id(0)
    tiles = pl.num_programs(0)
    key_span = NSEL * BLOCK
    width = grid_ref.shape[1]
    pair = 2 * (width // HEADS)
    base = lax.axis_index("tile") * tiles if owned else 0

    def fetch(which):
        slot = lax.rem(which, 2)

        def one(j, carry):
            spot = position_ref[list_ref[base + which, j]]
            pltpu.make_async_copy(
                blocks_ref.at[pl.ds(spot * BLOCK, BLOCK), :],
                raw.at[slot, pl.ds(j * BLOCK, BLOCK), :],
                copy_sem.at[slot],
            ).start()
            return carry

        lax.fori_loop(0, NSEL, one, 0)

    @pl.when(tile == 0)
    def _():
        fetch(tile)

    slot = lax.rem(tile, 2)
    pltpu.make_async_copy(
        blocks_ref.at[pl.ds(0, key_span), :], raw.at[slot], copy_sem.at[slot]
    ).wait()

    @pl.when(tile + 1 < tiles)
    def _():
        fetch(tile + 1)

    for start in range(0, key_span, CHUNK):
        rows = pl.ds(start, CHUNK)
        feats = raw[slot, rows, :].astype(jnp.float32)
        normed = ((feats - mean_ref[...]) * rstd_ref[...]).astype(jnp.bfloat16)
        hidden = jnp.dot(normed, w_obs_ref[...], preferred_element_type=jnp.float32)
        hidden = hidden + b_obs_ref[...]
        embedded = jax.nn.gelu(hidden, approximate=True).astype(jnp.bfloat16)
        keys[rows, :] = jnp.dot(
            embedded, w_key_ref[...], preferred_element_type=jnp.float32
        ).astype(jnp.bfloat16)
        values[rows, :] = jnp.dot(
            embedded, w_value_ref[...], preferred_element_type=jnp.float32
        ).astype(jnp.bfloat16)

    queries = jnp.dot(
        grid_ref[...], w_query_ref[...], preferred_element_type=jnp.float32
    ).astype(jnp.bfloat16)
    queries = queries * jnp.bfloat16(1.0 / (width // HEADS) ** 0.5)
    certain = 3 * key_span // 4
    used = count_ref[base + tile] * BLOCK
    key_index = certain + lax.broadcasted_iota(jnp.int32, (1, key_span - certain), 1)
    bias = jnp.where(key_index < used, 0.0, NEG).astype(jnp.float32)
    lane = lax.broadcasted_iota(jnp.int32, (TILE_ROWS, pair), 1)
    first = lane < pair // 2
    zero = jnp.zeros((), jnp.bfloat16)
    parts = []
    for p in range(HEADS // 2):
        columns = slice(p * pair, (p + 1) * pair)
        q = queries[:, columns]
        both = jnp.concatenate([jnp.where(first, q, zero), jnp.where(first, zero, q)], axis=0)
        scores = lax.dot_general(
            both,
            keys[:, columns],
            (((1,), (1,)), ((), ())),
            preferred_element_type=jnp.float32,
        )
        scores = jnp.concatenate([scores[:, :certain], scores[:, certain:] + bias], axis=1)
        peak = jnp.max(scores, axis=-1, keepdims=True)
        expo = jnp.exp(scores - peak)
        totals = jnp.sum(expo, axis=-1, keepdims=True)
        mixed = jnp.dot(
            expo.astype(jnp.bfloat16), values[:, columns], preferred_element_type=jnp.float32
        )
        mixed = mixed / totals
        parts.append(
            jnp.where(first, mixed[:TILE_ROWS], mixed[TILE_ROWS:]).astype(jnp.bfloat16)
        )
    attended = jnp.concatenate(parts, axis=1)
    encoded = jnp.dot(
        attended, w_out_ref[...], preferred_element_type=jnp.float32
    ).astype(jnp.bfloat16)
    out_ref[...] = encoded.reshape(out_ref.shape)


def attend(
    tile_count,
    owned,
    lists,
    counts,
    position,
    grid_tokens,
    blocks,
    mean,
    rstd,
    w_obs,
    b_obs,
    w_query,
    w_key,
    w_value,
    w_out,
):
    rows, width = grid_tokens.shape
    piece = TILE_ROWS // tile_count
    feat = blocks.shape[1]
    key_span = NSEL * BLOCK

    def whole(shape):
        return pl.BlockSpec(shape, lambda t, *_: (0, 0))

    square = whole((width, width))
    return pl.pallas_call(
        functools.partial(attend_kernel, owned),
        grid_spec=pltpu.PrefetchScalarGridSpec(
            num_scalar_prefetch=3,
            grid=(rows // TILE_ROWS,),
            in_specs=[
                pl.BlockSpec((TILE_ROWS, width), lambda t, *_: (t, 0)),
                pl.BlockSpec(memory_space=pl.ANY),
                whole((1, feat)),
                whole((1, feat)),
                whole((feat, width)),
                whole((1, width)),
                square,
                square,
                square,
                square,
            ],
            out_specs=pl.BlockSpec((tile_count, 1, piece, width), lambda t, *_: (0, t, 0, 0)),
            scratch_shapes=[
                pltpu.VMEM((2, key_span, feat), jnp.bfloat16),
                pltpu.VMEM((key_span, width), jnp.bfloat16),
                pltpu.VMEM((key_span, width), jnp.bfloat16),
                pltpu.SemaphoreType.DMA((2,)),
            ],
        ),
        out_shape=jax.ShapeDtypeStruct(
            (tile_count, rows // TILE_ROWS, piece, width), jnp.bfloat16
        ),
        compiler_params=pltpu.CompilerParams(dimension_semantics=("arbitrary",)),
        cost_estimate=pl.CostEstimate(
            flops=12_000_000_000, bytes_accessed=6_000_000, transcendentals=12_000_000
        ),
    )(
        lists,
        counts,
        position,
        grid_tokens,
        blocks,
        mean,
        rstd,
        w_obs,
        b_obs[None],
        w_query,
        w_key,
        w_value,
        w_out,
    )


MESH = pl.DeviceIdType.MESH


def greet_all(me, count):
    barrier = pltpu.get_barrier_semaphore()

    def one(k, carry):
        peer = lax.rem(me + k, count)
        pl.semaphore_signal(barrier, inc=1, device_id={"tile": peer}, device_id_type=MESH)
        return carry

    lax.fori_loop(1, count, one, 0)
    pl.semaphore_wait(barrier, count - 1)


LINES = 4
SIDES = LINES * 4
CORES = 2
PARTS = 1
STEP = 32
SUB = 4


def reorder(k, z):
    m = z // 2
    zz = z + m * (LINES - 1 - 2 * z)
    kk = k + zz * (1 - k // 2) * (1 - 2 * k)
    return kk + m * (LINES - 1 - 2 * kk)


def distance(zs, z):
    m = z // 2
    zz = z + m * (LINES - 1 - 2 * z)
    ss = zs + m * (LINES - 1 - 2 * zs)
    return ss + zz * (1 - ss // 2) * (1 - 2 * ss)


def plan_entries(me, lists_ref, count_ref, position_ref, plan, tiles, obs_blocks):
    entries = tiles * NSEL
    z, y = me // 4, lax.rem(me // 2, 2)
    shift = obs_blocks.bit_length() - 1
    lane = lax.broadcasted_iota(jnp.int32, lists_ref.shape, 1)
    row = lax.broadcasted_iota(jnp.int32, (NSEL, 1), 0)
    ids, used = [], []
    for t in range(tiles):
        tile = me * tiles + t
        ids.append(jnp.sum(jnp.where(lane == tile, lists_ref[...], 0), axis=1, keepdims=True))
        used.append((row < count_ref[tile]).astype(jnp.int32))
    ids = jnp.concatenate(ids, axis=0)
    used = jnp.concatenate(used, axis=0)
    blocks = position_ref.shape[1]
    which = lax.broadcasted_iota(jnp.int32, (entries, blocks), 1)
    spot = jnp.sum(jnp.where(ids == which, position_ref[...], 0), axis=1, keepdims=True)
    owner = lax.shift_right_logical(spot, shift)
    inner = spot & (obs_blocks - 1)
    oz = lax.shift_right_logical(owner, 2)
    oy = lax.shift_right_logical(owner, 1) & 1
    near = jnp.zeros_like(oz)
    for zs in range(LINES):
        near = jnp.where(oz == zs, distance(zs, z), near)
    slot = near * 4 + (oy ^ y) * 2 + (owner & 1)
    address = (slot * obs_blocks + inner) * used
    turn = jnp.where(slot == 7, 14, jnp.where((slot > 7) & (slot < 15), slot - 1, slot)) * used
    entry = lax.broadcasted_iota(jnp.int32, (entries, 1), 0)
    key = turn * entries + entry
    across = lax.broadcasted_iota(jnp.int32, (entries, entries), 1)
    down = lax.broadcasted_iota(jnp.int32, (entries, entries), 0)
    key_row = jnp.sum(jnp.where(across == down, key, 0), axis=0, keepdims=True)
    rank_row = jnp.sum((key < key_row).astype(jnp.int32), axis=0, keepdims=True)
    rank = jnp.sum((key_row < key).astype(jnp.int32), axis=1, keepdims=True)
    sorted_row = jnp.sum(jnp.where(rank == across, address, 0), axis=0, keepdims=True)
    plan[0:1, :] = rank_row
    plan[1:2, :] = sorted_row


def fused_kernel(
    lists_hbm,
    count_hbm,
    position_hbm,
    b_obs_hbm,
    obs_ref,
    grid_hbm,
    w_obs_hbm,
    w_query_hbm,
    w_key_hbm,
    w_value_hbm,
    w_out_hbm,
    arrived,
    land,
    ready,
    feed,
    lists_ref,
    count_ref,
    position_ref,
    b_obs_ref,
    grid_ref,
    w_obs_ref,
    w_query_ref,
    w_key_ref,
    w_value_ref,
    w_out_ref,
    keys,
    values,
    queries,
    encoded,
    plan,
    plan_s,
    tally,
    tallies,
    stats,
    sends,
    recvs,
    part_sends,
    part_recvs,
    out_sends,
    out_recvs,
    own_sems,
    stage_sems,
    load_sems,
    plan_sem,
    kept_sems,
):
    count = SIDES
    me = lax.axis_index("tile")
    z, y, c = me // 4, lax.rem(me // 2, 2), lax.rem(me, 2)
    rows = obs_ref.shape[0]
    half = rows // CORES
    bit = half // PARTS
    tokens, width = grid_ref.shape
    tiles = tokens // TILE_ROWS
    obs_blocks = rows
    pair = 2 * (width // HEADS)
    order = [reorder(k, z) for k in range(LINES)]
    middle = (z > 0) & (z < LINES - 1)
    edge = jnp.logical_not(middle)

    loads = [
        pltpu.make_async_copy(source, target, load_sems.at[i])
        for i, (source, target) in enumerate(
            (
                (lists_hbm, lists_ref),
                (count_hbm, count_ref),
                (position_hbm, position_ref),
                (b_obs_hbm, b_obs_ref),
                (grid_hbm, grid_ref),
                (w_query_hbm, w_query_ref),
                (w_obs_hbm, w_obs_ref),
                (w_key_hbm, w_key_ref),
                (w_value_hbm, w_value_ref),
                (w_out_hbm, w_out_ref),
            )
        )
    ]
    own_place = pl.ds(pl.multiple_of(c * rows, rows), rows)
    own_copies = [
        pltpu.make_async_copy(obs_ref, ref.at[own_place], own_sems.at[i])
        for i, ref in enumerate((ready, land))
    ]

    def index(zz, yy, cc):
        return (zz * 2 + yy) * 2 + cc

    def slot_of(source, zt, yt):
        zs, ys, cs = source
        return distance(zs, zt) * 4 + lax.rem(ys + yt, 2) * 2 + cs

    def span(slot, side, part):
        return pl.ds(pl.multiple_of(slot * rows + side * half + part * bit, bit), bit)

    def send(source, target, side, part, way, own=False):
        block = index(*source)
        piece = (block * CORES + side) * PARTS + part
        return pltpu.make_async_remote_copy(
            src_ref=obs_ref.at[pl.ds(pl.multiple_of(side * half + part * bit, bit), bit)]
            if own
            else land.at[span(slot_of(source, z, y), side, part)],
            dst_ref=land.at[span(slot_of(source, target[0], target[1]), side, part)],
            send_sem=sends.at[way, piece],
            recv_sem=recvs.at[piece],
            device_id={"tile": index(*target)},
            device_id_type=MESH,
        )

    started = []

    def launch(source, target, side, part, way, own=False, when=None):
        def issue(finish):
            def go():
                copy = send(source(), target(), side(), part, way, own)
                copy.wait_send() if finish else copy.start()

            if when is None:
                go()
            else:
                pl.when(when())(go)

        started.append(issue)
        issue(False)

    def below_me():
        return z - 1, y, c

    def above_me():
        return z + 1, y, c

    def to_across():
        return z, 1 - y, c

    def to_beside():
        return z, y, 1 - c

    def my_side():
        return c

    def other_side():
        return 1 - c

    def arrive(source, side, part):
        send(source, to_beside(), side, part, 3).wait_recv()

    def spread(source, own, when):
        def both(cond):
            return cond if when is None else lambda: when() & cond()

        for part in range(PARTS):
            launch(source, below_me, my_side, part, 0, own, both(lambda: z > 0))
            launch(source, above_me, my_side, part, 1, own, both(lambda: z < LINES - 1))
            launch(source, to_across, my_side, part, 2, own, when)

    for copy in own_copies + loads:
        copy.start()
    greet_all(me, count)
    for part in range(PARTS):
        launch(lambda: (z, y, c), to_beside, other_side, part, 3, True)
    spread(lambda: (z, y, 0), True, lambda: c == 0)

    @pl.when(c == 1)
    def _():
        for part in range(PARTS):
            arrive((z, y, 0), c, part)

    spread(lambda: (z, y, 0), False, lambda: c == 1)

    @pl.when(c == 0)
    def _():
        for part in range(PARTS):
            arrive((z, y, 1), c, part)

    spread(lambda: (z, y, 1), False, lambda: c == 0)
    spread(lambda: (z, y, 1), True, lambda: c == 1)
    for part in range(PARTS):
        launch(lambda: (z, y, c), to_beside, my_side, part, 3, True)

    own_copies[0].wait()
    feats = ready[own_place].reshape(rows * BLOCK, obs_ref.shape[2]).astype(jnp.float32)
    tally[...] = jnp.zeros_like(tally)
    tally[0:1, :] = jnp.sum(feats, axis=0, keepdims=True)
    tally[1:2, :] = jnp.sum(feats * feats, axis=0, keepdims=True)
    tallies[pl.ds(me, 1)] = tally[...][None]

    def share_copy(k, source, peer):
        return pltpu.make_async_remote_copy(
            src_ref=tally,
            dst_ref=tallies.at[source],
            send_sem=part_sends.at[k],
            recv_sem=part_recvs.at[source],
            device_id={"tile": peer},
            device_id_type=MESH,
        )

    def share(k, carry):
        share_copy(k, me, lax.rem(me + k, count)).start()
        return carry

    lax.fori_loop(1, count, share, 0)

    for copy in loads[:6]:
        copy.wait()
    plan_entries(me, lists_ref, count_ref, position_ref, plan, tiles, obs_blocks)
    plan_copy = pltpu.make_async_copy(plan, plan_s, plan_sem)
    plan_copy.start()
    queries[...] = jnp.dot(
        grid_ref[...], w_query_ref[...], preferred_element_type=jnp.float32
    ).astype(jnp.bfloat16) * jnp.bfloat16(1.0 / (width // HEADS) ** 0.5)
    plan_copy.wait()

    def column(k, cc):
        def source():
            return order[k], y, cc

        for part in range(PARTS):
            arrive(source(), c, part)
            launch(source, below_me, my_side, part, 0, False, lambda: (order[k] > z) & (z > 0))
            launch(source, above_me, my_side, part, 1, False, lambda: (order[k] < z) & (z < LINES - 1))
            if not (k == 1 and cc == 1):
                launch(source, to_across, my_side, part, 2)
            launch(source, to_beside, my_side, part, 3)

    def opposite(k, cc):
        def source():
            return order[k], 1 - y, cc

        for part in range(PARTS):
            arrive(source(), c, part)
            launch(source, to_beside, my_side, part, 3)

    def level():
        for part in range(PARTS):
            launch(lambda: (z, 1 - y, 1), lambda: (order[1], y, c), my_side, part, 4)

    def twin(k, dy, cc):
        for part in range(PARTS):
            arrive((order[k], lax.rem(y + dy, 2), cc), 1 - c, part)

    def kinds(inner, outer):
        kept = len(started)

        @pl.when(middle)
        def _():
            for event, args in inner:
                event(*args)

        del started[kept:]

        @pl.when(edge)
        def _():
            for event, args in outer:
                event(*args)

    def stage(sem, first, last):
        place = pl.ds(first * rows, (last - first) * rows)
        return pltpu.make_async_copy(land.at[place], ready.at[place], stage_sems.at[sem])

    for part in range(PARTS):
        arrive((z, y, 1 - c), 1 - c, part)
    beside_place = pl.ds(pl.multiple_of((1 - c) * rows, rows), rows)
    beside_copy = pltpu.make_async_copy(land.at[beside_place], ready.at[beside_place], stage_sems.at[0])
    beside_copy.start()
    columns = [(column, (1, 0)), (column, (1, 1)), (column, (2, 0)), (column, (2, 1))]
    columns += [(column, (3, 0)), (column, (3, 1))]
    across = [(opposite, (0, 0)), (opposite, (0, 1)), (opposite, (1, 0)), (opposite, (2, 0))]
    rebalance = (level, ())
    inner = [columns[0], columns[2], across[0], columns[1], columns[3], across[1]]
    inner += [columns[4], across[2], columns[5], rebalance, across[3]]
    outer = [columns[0], across[0], columns[1], across[1], rebalance]
    outer += [columns[2], across[2], columns[3], across[3]]
    kinds(inner, outer)
    for k, dy, cc in ((0, 1, 0), (0, 1, 1), (1, 0, 0), (1, 0, 1), (1, 1, 0)):
        twin(k, dy, cc)
    stage(1, 2, 7).start()
    for k, dy, cc in ((2, 0, 0), (2, 0, 1), (2, 1, 0)):
        twin(k, dy, cc)
    stage(2, 8, 11).start()

    def gathered(k, carry):
        peer = lax.rem(me + k, count)
        share_copy(k, peer, peer).wait_send()
        share_copy(k, peer, peer).wait_recv()
        return carry

    lax.fori_loop(1, count, gathered, 0)
    sums = jnp.sum(tallies[...], axis=0)
    total = rows * BLOCK * count
    mean = sums[0:1, :] / total
    stats[0:1, :] = mean
    stats[1:2, :] = lax.rsqrt(sums[1:2, :] / total - mean * mean + 1e-05)

    own_copies[1].wait()
    beside_copy.wait()
    stage(1, 2, 7).wait()
    stage(2, 8, 11).wait()
    for copy in loads[6:]:
        copy.wait()

    chunks = tiles * NSEL // STEP
    share_of = chunks // 4

    def advance(sem, first, last):
        copy = stage(sem, first, last)
        copy.start()
        copy.wait()

    def chunk(i, carry):
        @pl.when(i == share_of)
        def _():
            opposite(2, 1)
            kinds([], [columns[4]])
            twin(2, 1, 1)
            twin(3, 0, 0)
            advance(3, 11, 13)

        @pl.when(i == 2 * share_of)
        def _():
            kinds([], [columns[5]])
            opposite(3, 0)
            twin(3, 1, 0)
            twin(3, 0, 1)
            advance(4, 13, 15)

        @pl.when(i == 3 * share_of)
        def _():
            opposite(3, 1)
            opposite(1, 1)
            twin(3, 1, 1)
            twin(1, 1, 1)

        @pl.when(i < 3 * share_of)
        def _():
            for u in range(STEP):
                feed[u] = ready[plan_s[1, i * STEP + u]]

        @pl.when(i >= 3 * share_of)
        def _():
            for u in range(STEP):
                feed[u] = land[plan_s[1, i * STEP + u]]

        def embed(n):
            feats = feed[n * SUB : (n + 1) * SUB].reshape(SUB * BLOCK, feed.shape[2])
            normed = (feats.astype(jnp.float32) - stats[0:1, :]) * stats[1:2, :]
            hidden = jnp.dot(
                normed.astype(jnp.bfloat16), w_obs_ref[...], preferred_element_type=jnp.float32
            )
            hidden = hidden + b_obs_ref[...]
            return jax.nn.gelu(hidden, approximate=True).astype(jnp.bfloat16)

        ahead = embed(0)
        for n in range(STEP // SUB):
            embedded = ahead
            if n + 1 < STEP // SUB:
                ahead = embed(n + 1)
            place = pl.ds(i * STEP + n * SUB, SUB)
            key_rows = jnp.dot(embedded, w_key_ref[...], preferred_element_type=jnp.float32)
            keys[place] = key_rows.astype(jnp.bfloat16).reshape(SUB, BLOCK, width)
            value_rows = jnp.dot(embedded, w_value_ref[...], preferred_element_type=jnp.float32)
            values[place] = value_rows.astype(jnp.bfloat16).reshape(SUB, BLOCK, width)
        return carry

    lax.fori_loop(0, chunks, chunk, 0)

    key_span = NSEL * BLOCK
    certain = 3 * key_span // 4
    first = lax.broadcasted_iota(jnp.int32, (TILE_ROWS, pair), 1) < pair // 2
    zero = jnp.zeros((), jnp.bfloat16)
    piece = TILE_ROWS // count

    def out_copy(t, source, peer):
        return pltpu.make_async_remote_copy(
            src_ref=encoded.at[t, peer],
            dst_ref=arrived.at[source * tiles + t],
            send_sem=out_sends,
            recv_sem=out_recvs,
            device_id={"tile": peer},
            device_id_type=MESH,
        )

    def kept_copy(t):
        return pltpu.make_async_copy(
            encoded.at[t, me], arrived.at[me * tiles + t], kept_sems.at[t]
        )

    def attend_tile(t, carry):
        used = count_ref[me * tiles + t] * BLOCK
        key_index = certain + lax.broadcasted_iota(jnp.int32, (1, key_span - certain), 1)
        bias = jnp.where(key_index < used, 0.0, NEG).astype(jnp.float32)
        places = [plan_s[0, t * NSEL + j] for j in range(NSEL)]
        outs = []

        def score(p):
            columns = slice(p * pair, (p + 1) * pair)
            q = queries[pl.ds(pl.multiple_of(t * TILE_ROWS, TILE_ROWS), TILE_ROWS), columns]
            both = jnp.concatenate([jnp.where(first, q, zero), jnp.where(first, zero, q)], axis=0)
            key_rows = jnp.concatenate([keys[place, :, columns] for place in places], axis=0)
            scores = lax.dot_general(
                both, key_rows, (((1,), (1,)), ((), ())), preferred_element_type=jnp.float32
            )
            return jnp.concatenate([scores[:, :certain], scores[:, certain:] + bias], axis=1)

        ahead = score(0)
        for p in range(HEADS // 2):
            scores = ahead
            if p + 1 < HEADS // 2:
                ahead = score(p + 1)
            columns = slice(p * pair, (p + 1) * pair)
            value_rows = jnp.concatenate([values[place, :, columns] for place in places], axis=0)
            value_rows = jnp.concatenate([value_rows, jnp.ones_like(value_rows)], axis=1)
            peak = jnp.max(scores, axis=-1, keepdims=True)
            expo = jnp.exp(scores - peak).astype(jnp.bfloat16)
            mixed = jnp.dot(expo, value_rows, preferred_element_type=jnp.float32)
            mixed = mixed[:, :pair] / mixed[:, pair:]
            outs.append(jnp.where(first, mixed[:TILE_ROWS], mixed[TILE_ROWS:]).astype(jnp.bfloat16))
        attended = jnp.concatenate(outs, axis=1)
        result = jnp.dot(attended, w_out_ref[...], preferred_element_type=jnp.float32)
        encoded[t] = result.astype(jnp.bfloat16).reshape(count, piece, width)

        def start(k, carry):
            out_copy(t, me, lax.rem(me + k, count)).start()
            return carry

        lax.fori_loop(1, count, start, 0, unroll=5)
        kept_copy(t).start()
        return carry

    lax.fori_loop(0, tiles, attend_tile, 0)

    for issue in started:
        issue(True)

    for sem in (out_sends, out_recvs):
        moved = arrived.at[pl.ds(0, tiles * (count - 1))]
        pltpu.make_async_copy(moved, moved, sem).wait()

    for t in range(tiles):
        kept_copy(t).wait()


def arrange_kernel(order_ref, arrived, out):
    for j in range(out.shape[0]):
        out[j] = arrived[order_ref[j]]


def arrange(arrived, proc_order):
    vmem = pl.BlockSpec(memory_space=pltpu.VMEM)
    return pl.pallas_call(
        arrange_kernel,
        out_shape=jax.ShapeDtypeStruct(arrived.shape, arrived.dtype),
        in_specs=[pl.BlockSpec(memory_space=pltpu.SMEM), vmem],
        out_specs=vmem,
    )(proc_order, arrived)


def fused(lists, counts, position, proc_order, grid_tokens, obs_features, w_obs, b_obs, w_query, w_key, w_value, w_out):
    tokens, width = grid_tokens.shape
    rows, feat = obs_features.shape[0] // BLOCK, obs_features.shape[1]
    tiles = tokens // TILE_ROWS
    count = SIDES
    piece = TILE_ROWS // count
    entries = tiles * NSEL
    shape = (count * tiles, piece, width)
    bf16 = jnp.bfloat16
    dma = pltpu.SemaphoreType.DMA
    arrived = pl.pallas_call(
        fused_kernel,
        out_shape=jax.ShapeDtypeStruct(shape, bf16),
        in_specs=[pl.BlockSpec(memory_space=pltpu.HBM)] * 11,
        out_specs=pl.BlockSpec(memory_space=pltpu.HBM),
        scratch_shapes=[
            pltpu.VMEM((SIDES * rows, BLOCK, feat), bf16),
            pltpu.VMEM(((SIDES - 1) * rows, BLOCK, feat), bf16),
            pltpu.VMEM((STEP, BLOCK, feat), bf16),
            pltpu.VMEM((NSEL, count * tiles), jnp.int32),
            pltpu.SMEM(counts.shape, jnp.int32),
            pltpu.VMEM((1, position.shape[0]), jnp.int32),
            pltpu.VMEM((1, width), jnp.float32),
            pltpu.VMEM((tokens, width), bf16),
            pltpu.VMEM((feat, width), bf16),
            pltpu.VMEM((width, width), bf16),
            pltpu.VMEM((width, width), bf16),
            pltpu.VMEM((width, width), bf16),
            pltpu.VMEM((width, width), bf16),
            pltpu.VMEM((entries, BLOCK, width), bf16),
            pltpu.VMEM((entries, BLOCK, width), bf16),
            pltpu.VMEM((tokens, width), bf16),
            pltpu.VMEM((tiles, count, piece, width), bf16),
            pltpu.VMEM((8, entries), jnp.int32),
            pltpu.SMEM((8, entries), jnp.int32),
            pltpu.VMEM((8, feat), jnp.float32),
            pltpu.VMEM((count, 8, feat), jnp.float32),
            pltpu.VMEM((8, feat), jnp.float32),
            dma((5, count * CORES * PARTS)),
            dma((count * CORES * PARTS,)),
            dma((count,)),
            dma((count,)),
            dma,
            dma,
            dma((2,)),
            dma((5,)),
            dma((10,)),
            dma,
            dma((tiles,)),
        ],
        compiler_params=pltpu.CompilerParams(
            collective_id=0, has_side_effects=True, vmem_limit_bytes=62 * 2**20
        ),
    )(
        lists.T,
        counts,
        position[None],
        b_obs[None],
        obs_features.reshape(rows, BLOCK, feat),
        grid_tokens,
        w_obs,
        w_query,
        w_key,
        w_value,
        w_out,
    )
    return arrange(arrived, proc_order).reshape(count * tiles * piece, width)


def exchange(obs_features, block_lists, block_counts, block_position, tile_count, own_index):
    obs_blocks = obs_features.shape[0] // BLOCK
    tile_local = block_lists.shape[0] // tile_count
    entry_count = tile_local * NSEL
    capacity = max(2, 2 * entry_count // tile_count)
    spots = jnp.take(block_position, block_lists, axis=0)
    is_valid = jnp.arange(NSEL, dtype=jnp.int32)[None, :] < block_counts[:, None]
    owner_dev = (spots // obs_blocks).reshape(tile_count, entry_count)
    local_blk = (spots % obs_blocks).reshape(tile_count, entry_count)
    valid_rows = is_valid.reshape(tile_count, entry_count)
    entry_order = jnp.arange(entry_count, dtype=jnp.int32)
    earlier = (
        (owner_dev[:, :, None] == owner_dev[:, None, :])
        & valid_rows[:, None, :]
        & (entry_order[None, :] < entry_order[:, None])[None, :, :]
    )
    slot_rank = jnp.sum(earlier.astype(jnp.int32), axis=2)
    mine = valid_rows & (owner_dev == own_index)
    slot_ids = jnp.arange(capacity, dtype=jnp.int32)
    hits = mine[:, None, :] & (slot_rank[:, None, :] == slot_ids[None, :, None])
    slot_block = jnp.sum(jnp.where(hits, local_blk[:, None, :], 0), axis=2)
    my_owner = lax.dynamic_index_in_dim(owner_dev, own_index, 0, keepdims=False)
    my_rank = lax.dynamic_index_in_dim(slot_rank, own_index, 0, keepdims=False)
    my_valid = lax.dynamic_index_in_dim(valid_rows, own_index, 0, keepdims=False)
    pick = jnp.where(my_valid, my_owner * capacity + my_rank, 0)
    raw_blocks = obs_features.reshape(obs_blocks, BLOCK, obs_features.shape[1])
    chosen = slot_block.reshape(-1, 1) == jnp.arange(obs_blocks, dtype=jnp.int32)[None, :]
    outgoing = jnp.einsum(
        "sb,brf->srf",
        chosen.astype(raw_blocks.dtype),
        raw_blocks,
        preferred_element_type=jnp.float32,
    ).astype(raw_blocks.dtype)
    incoming = lax.all_to_all(outgoing, "tile", split_axis=0, concat_axis=0, tiled=True)
    return incoming.reshape(tile_count * capacity * BLOCK, obs_features.shape[1]), pick


def local(
    grid_tokens,
    obs_features,
    w_obs,
    b_obs,
    w_query,
    w_key,
    w_value,
    w_out,
    block_lists,
    block_counts,
    block_position,
    proc_order,
):
    tile_count = lax.axis_size("tile")
    own_index = lax.axis_index("tile")
    tile_local = grid_tokens.shape[0] // TILE_ROWS
    width = grid_tokens.shape[1]
    if tile_count == SIDES:
        return fused(
            block_lists,
            block_counts,
            block_position,
            proc_order,
            grid_tokens,
            obs_features,
            w_obs,
            b_obs,
            w_query,
            w_key,
            w_value,
            w_out,
        )
    obs_wide = obs_features.astype(jnp.float32)
    first_sum, second_sum = lax.psum(
        (
            jnp.sum(obs_wide, axis=0, keepdims=True),
            jnp.sum(obs_wide * obs_wide, axis=0, keepdims=True),
        ),
        "tile",
    )
    obs_total = obs_features.shape[0] * tile_count
    feat_mean = first_sum / obs_total
    feat_rstd = lax.rsqrt(second_sum / obs_total - feat_mean * feat_mean + 1e-05)
    blocks, pick = exchange(
        obs_features, block_lists, block_counts, block_position, tile_count, own_index
    )
    encoded = attend(
        1,
        False,
        pick.reshape(tile_local, NSEL),
        lax.dynamic_slice_in_dim(block_counts, own_index * tile_local, tile_local),
        jnp.arange(blocks.shape[0] // BLOCK, dtype=jnp.int32),
        grid_tokens,
        blocks,
        feat_mean,
        feat_rstd,
        w_obs,
        b_obs,
        w_query,
        w_key,
        w_value,
        w_out,
    )
    outgoing = encoded.reshape(tile_local, tile_count, TILE_ROWS // tile_count, width)
    arrived = lax.all_to_all(outgoing, "tile", split_axis=1, concat_axis=0, tiled=True)
    arrived = arrived.reshape(tile_count * tile_local, TILE_ROWS // tile_count, width)
    return jnp.take(arrived, proc_order, axis=0).reshape(
        tile_count * tile_local * (TILE_ROWS // tile_count), width
    )


def solution(mesh):
    in_specs = (
        P(("groups", "tile"), None),
        P(("groups", "tile"), None),
        P(),
        P(),
        P(),
        P(),
        P(),
        P(),
        P("groups", None),
        P("groups"),
        P("groups"),
        P("groups"),
    )
    out_specs = P(("groups", "tile"), None)
    return jax.shard_map(local, mesh=mesh, in_specs=in_specs, out_specs=out_specs, check_vma=False)
```
